32 devices in a mesh: group: 4 (over y, x), space: 8 (over z, core).
Axes of the slice: x: 2, y: 2, z: 4, core: 2. Of those that a mesh axis runs over, the one named last changes fastest.
Arguments:
- vectors: bfloat16 [128, 2, 3, 4096], P('group', None, None, 'space'), may hold values from -3 to 3
- momentum: int32 [3], replicated, may hold values from -3 to 3
- assignment: int32 [128], replicated, may hold values from 0 to 127, each once
Outputs:
- elementals: float32 [128, 2, 128, 128], P('space', None, 'group')
The draws below stay inside these ranges and needn't reach their ends.
Inputs may be any that keep to these rules, and one draw needn't show every extreme that they name: `assignment`: each eigenvector is named by exactly one slot.
All inputs are finite; a program needn't handle non-finite values.
Results may differ from the reference program's by a relative error of at most 0.0029.
Values may be sent and summed in bfloat16 or wider, within the bound.
A program may use at most 128 MiB of HBM per device.

```python
import math
import jax
import jax.numpy as jnp
from jax import lax

N = 128
L = 64
SITES = 4096


def levels(key, extent, split, low, high):
    gain = 1.0
    for dim, shards_of in split:
        heights = jax.random.uniform(jax.random.fold_in(jax.random.fold_in(key, 6), dim), (shards_of,), jnp.float32, low / len(split), high / len(split))
        gain = gain * jnp.repeat(jnp.exp(heights), extent[dim] // shards_of).reshape((-1,) + (1,) * (len(extent) - 1 - dim))
    return gain


def normal_values(rng, dims, scale, bound, split=(), kind=jnp.bfloat16):
    loudness = levels(rng, dims, split, -0.22, 0.18) if split else 1.0
    drawn = jax.random.normal(rng, dims, jnp.float32) * scale * loudness
    return jnp.minimum(jnp.maximum(drawn, -bound), bound).astype(kind)


def setup_inputs(seed: int = 0) -> dict:
    arg_keys = jax.random.split(jax.random.key(seed), 4)
    vectors = normal_values(arg_keys[0], (N, 2, 3, SITES), 0.5, 3.0, ((0, 4), (3, 8)))
    momentum = jax.random.randint(arg_keys[1], (3,), -3, 4).astype(jnp.int32)
    assignment = jax.random.permutation(arg_keys[2], N).astype(jnp.int32)
    return dict(vectors=vectors, momentum=momentum, assignment=assignment)


def complex_product(left_re, left_im, right_re, right_im):
    return (left_re * right_re - left_im * right_im, left_re * right_im + left_im * right_re)

def weighted_slot(vec32, slot_vec, cosine, sine):
    crosses_re = []
    crosses_im = []
    for colour in range(3):
        second = (colour + 1) % 3
        third = (colour + 2) % 3
        one_re, one_im = complex_product(vec32[:, 0, second], vec32[:, 1, second], slot_vec[0, third], slot_vec[1, third])
        two_re, two_im = complex_product(vec32[:, 0, third], vec32[:, 1, third], slot_vec[0, second], slot_vec[1, second])
        cross_re = one_re - two_re
        cross_im = one_im - two_im
        crosses_re.append(cross_re * cosine - cross_im * sine)
        crosses_im.append(cross_re * sine + cross_im * cosine)
    stacked = jnp.stack([jnp.stack(crosses_re, axis=1), jnp.stack(crosses_im, axis=1)], axis=1)
    return stacked.astype(jnp.bfloat16)

def reference(vectors, momentum, assignment):
    sites = jnp.arange(SITES, dtype=jnp.int32)
    coord_x = sites % L
    coord_y = sites // L % L
    coord_z = sites // (L * L)
    phase_index = jnp.mod(momentum[0] * coord_x + momentum[1] * coord_y + momentum[2] * coord_z, L).astype(jnp.int32)
    angle = phase_index.astype(jnp.float32) * jnp.float32(2.0 * math.pi / L)
    cosine = jnp.cos(angle)
    sine = jnp.sin(angle)
    vec32 = vectors.astype(jnp.float32)
    flat_left = vec32.reshape(N, 2, 3 * SITES)

    def one_slot(index):
        slot_vec = vec32[index]
        weighted = weighted_slot(vec32, slot_vec, cosine, sine).astype(jnp.float32).reshape(N, 2, 3 * SITES)
        products = jnp.einsum('ipx,jqx->ipqj', flat_left, weighted)
        real_part = products[:, 0, 0] - products[:, 1, 1]
        imag_part = products[:, 0, 1] + products[:, 1, 0]
        return jnp.stack([real_part, imag_part], axis=1)
    slots = lax.map(one_slot, assignment)
    scale = 1.0 / math.sqrt(SITES)
    return jnp.transpose(slots, (1, 2, 0, 3)) * jnp.float32(scale)
```

```python
import functools
import math

import jax
import jax.numpy as jnp
from jax import lax
from jax.experimental import pallas as pl
from jax.experimental.pallas import tpu as pltpu
from jax.sharding import PartitionSpec as P

L = 64
MESH = pl.DeviceIdType.MESH
LANES = 128
ROWS = 16
SLOTS = 4


def general_kernel(
    groups,
    spaces,
    slots_ref,
    momentum_ref,
    block_ref,
    out_ref,
    gathered,
    wide,
    right,
    weighted,
    part,
    pair_out,
    part_in,
    rounded,
    rounded_in,
    local_sem,
    gather_send,
    gather_recv,
    pair_send,
    pair_recv,
    sum_send,
    sum_recv,
):
    block = block_ref.shape[1]
    site_count = block_ref.shape[2]
    total = groups * block
    rows = total // spaces
    planes = spaces // 2
    steps = block // SLOTS
    span = 3 * site_count
    scale = jnp.float32(1.0 / math.sqrt(site_count * spaces))
    group = lax.axis_index("group")
    space = lax.axis_index("space")
    core = lax.rem(space, 2)
    plane = lax.div(space, 2)

    barrier = pltpu.get_barrier_semaphore()
    for off in range(1, groups):
        pl.semaphore_signal(
            barrier, inc=1, device_id={"group": lax.rem(group + off, groups)}, device_id_type=MESH
        )
    for off in range(1, planes):
        pl.semaphore_signal(
            barrier,
            inc=1,
            device_id={"space": lax.rem(plane + off, planes) * 2 + core},
            device_id_type=MESH,
        )
    pl.semaphore_signal(
        barrier, inc=1, device_id={"space": plane * 2 + 1 - core}, device_id_type=MESH
    )
    pl.semaphore_wait(barrier, groups + planes - 1)

    def gather_copy(lane, target, source, owner, first, count):
        at = pl.ds(first, count)
        return pltpu.make_async_remote_copy(
            src_ref=source.at[at],
            dst_ref=gathered.at[owner, at],
            send_sem=gather_send.at[lane],
            recv_sem=gather_recv.at[lane],
            device_id={"group": target},
            device_id_type=MESH,
        )

    square = groups == 4
    if square:
        beside = group + 1 - 2 * lax.rem(group, 2)
        across = group + 2 - 4 * lax.div(group, 2)
        sends = [
            gather_copy(0, beside, block_ref, group, 0, 3),
            gather_copy(1, across, block_ref, group, 3, 3),
            gather_copy(2, beside, block_ref, group, 3, 3),
            gather_copy(3, across, block_ref, group, 0, 3),
        ]
        passed = [
            gather_copy(4, across, gathered.at[beside], beside, 0, 3),
            gather_copy(5, beside, gathered.at[across], across, 3, 3),
        ]
    else:
        sends = [
            gather_copy(off - 1, lax.rem(group + off, groups), block_ref, group, 0, 6)
            for off in range(1, groups)
        ]
    for copy in sends:
        copy.start()
    own = pltpu.make_async_copy(block_ref, gathered.at[group], local_sem)
    own.start()
    if square:
        for copy, onward in zip(sends, passed):
            copy.wait_recv()
            onward.start()

    sites = space * site_count + lax.broadcasted_iota(jnp.int32, (8, site_count), 1)
    coord_x = sites & (L - 1)
    coord_y = (sites >> 6) & (L - 1)
    coord_z = sites >> 12
    phase = momentum_ref[0] * coord_x + momentum_ref[1] * coord_y + momentum_ref[2] * coord_z
    angle = (phase & (L - 1)).astype(jnp.float32) * jnp.float32(2.0 * math.pi / L)
    cosine = jnp.cos(angle)[0:1]
    sine = jnp.sin(angle)[0:1]

    own.wait()
    if square:
        for copy in sends[:2]:
            copy.wait_send()
        for copy in sends[2:] + passed:
            copy.wait()
    else:
        for copy in sends:
            copy.wait()

    for q in range(groups):
        for c in range(6):
            wide[c, q * block : (q + 1) * block, :] = gathered[q, c].astype(jnp.float32)

    for a in range(3):
        real = wide[a].T.astype(jnp.bfloat16)
        imag = wide[3 + a].T.astype(jnp.bfloat16)
        low, high = a * site_count, (a + 1) * site_count
        right[low:high, :total] = real
        right[low:high, total:] = imag
        right[span + low : span + high, :total] = -imag
        right[span + low : span + high, total:] = real

    def fill(step, first, stop):
        def one(half, carry):
            k = slots_ref[group * block + SLOTS * step + half]
            row = [wide[c, pl.ds(k, 1), :] for c in range(6)]
            turn_re = [row[a] * cosine - row[3 + a] * sine for a in range(3)]
            turn_im = [row[a] * sine + row[3 + a] * cosine for a in range(3)]

            def tile(j, inner):
                top = pl.multiple_of(j * ROWS, ROWS)
                for s in range(0, site_count, LANES):
                    cols = slice(s, s + LANES)
                    re = [wide[a, pl.ds(top, ROWS), cols] for a in range(3)]
                    im = [wide[3 + a, pl.ds(top, ROWS), cols] for a in range(3)]
                    tr = [x[:, cols] for x in turn_re]
                    ti = [x[:, cols] for x in turn_im]
                    for a in range(3):
                        b, c = (a + 1) % 3, (a + 2) % 3
                        out_re = (re[b] * tr[c] - im[b] * ti[c]) - (re[c] * tr[b] - im[c] * ti[b])
                        out_im = (re[b] * ti[c] + im[b] * tr[c]) - (re[c] * ti[b] + im[c] * tr[b])
                        base = a * site_count + s
                        at = pl.ds(pl.multiple_of(half * total + top, ROWS), ROWS)
                        weighted[at, base : base + LANES] = out_re.astype(jnp.bfloat16)
                        weighted[at, span + base : span + base + LANES] = out_im.astype(jnp.bfloat16)
                return inner

            return lax.fori_loop(0, total // ROWS, tile, carry, unroll=True)

        lax.fori_loop(first, stop, one, 0)

    def pair_copy(step):
        return pltpu.make_async_remote_copy(
            src_ref=pair_out.at[step],
            dst_ref=part_in.at[step],
            send_sem=pair_send.at[step],
            recv_sem=pair_recv.at[step],
            device_id={"space": plane * 2 + 1 - core},
            device_id_type=MESH,
        )

    def sum_copy(step, off):
        target = lax.rem(plane + off, planes)
        return pltpu.make_async_remote_copy(
            src_ref=rounded.at[step, target],
            dst_ref=rounded_in.at[off - 1, step],
            send_sem=sum_send.at[off - 1, step],
            recv_sem=sum_recv.at[off - 1, step],
            device_id={"space": target * 2 + core},
            device_id_type=MESH,
        )

    def forward(step):
        pair_copy(step).wait()
        rounded[step] = (part[step, core] + part_in[step].astype(jnp.float32)).astype(jnp.bfloat16)
        for off in range(1, planes):
            sum_copy(step, off).start()
        out_ref[pl.ds(SLOTS * step, SLOTS)] = part[step, core, plane] + part_in[step, plane].astype(jnp.float32)

    def body(step, carry):
        fill(step, 0, SLOTS - 1)

        @pl.when(step >= 1)
        def _():
            forward(step - 1)

        fill(step, SLOTS - 1, SLOTS)
        product = jnp.dot(weighted[...], right[...], preferred_element_type=jnp.float32)
        for half in range(SLOTS):
            piece = product[half * total : (half + 1) * total].T
            for c in range(2):
                for i in range(spaces):
                    first = c * total + i * rows
                    part[step, i % 2, i // 2, half, c * rows : (c + 1) * rows] = piece[
                        first : first + rows
                    ]
        pair_out[step] = part[step, 1 - core].astype(jnp.bfloat16)
        pair_copy(step).start()

        return carry

    lax.fori_loop(0, steps, body, 0)
    forward(steps - 1)

    def finish(step, carry):
        value = out_ref[pl.ds(SLOTS * step, SLOTS)]
        for off in range(1, planes):
            sum_copy(step, off).wait()
            value = value + rounded_in[off - 1, step].astype(jnp.float32)
        out_ref[pl.ds(SLOTS * step, SLOTS)] = value * scale
        return carry

    lax.fori_loop(0, steps, finish, 0)


def general(groups, spaces, vectors, momentum, assignment):
    block, _, _, site_count = vectors.shape
    total = block * groups
    rows = total // spaces
    planes = spaces // 2
    steps = block // SLOTS
    mine = jnp.transpose(vectors, (1, 2, 0, 3)).reshape(6, block, site_count)
    dma = pltpu.SemaphoreType.DMA
    out = pl.pallas_call(
        functools.partial(general_kernel, groups, spaces),
        out_shape=jax.ShapeDtypeStruct((block, 2 * rows, total), jnp.float32),
        in_specs=[
            pl.BlockSpec(memory_space=pltpu.SMEM),
            pl.BlockSpec(memory_space=pltpu.SMEM),
            pl.BlockSpec(memory_space=pltpu.VMEM),
        ],
        out_specs=pl.BlockSpec(memory_space=pltpu.VMEM),
        scratch_shapes=[
            pltpu.VMEM((groups, 6, block, site_count), jnp.bfloat16),
            pltpu.VMEM((6, total, site_count), jnp.float32),
            pltpu.VMEM((6 * site_count, 2 * total), jnp.bfloat16),
            pltpu.VMEM((SLOTS * total, 6 * site_count), jnp.bfloat16),
            pltpu.VMEM((steps, 2, planes, SLOTS, 2 * rows, total), jnp.float32),
            pltpu.VMEM((steps, planes, SLOTS, 2 * rows, total), jnp.bfloat16),
            pltpu.VMEM((steps, planes, SLOTS, 2 * rows, total), jnp.bfloat16),
            pltpu.VMEM((steps, planes, SLOTS, 2 * rows, total), jnp.bfloat16),
            pltpu.VMEM((planes - 1, steps, SLOTS, 2 * rows, total), jnp.bfloat16),
            dma,
            dma((max(groups - 1, 6),)),
            dma((max(groups - 1, 6),)),
            dma((steps,)),
            dma((steps,)),
            dma((planes - 1, steps)),
            dma((planes - 1, steps)),
        ],
        compiler_params=pltpu.CompilerParams(
            collective_id=0, has_side_effects=True, vmem_limit_bytes=48 * 1024 * 1024
        ),
    )(assignment, momentum, mine)
    return jnp.transpose(out.reshape(block, 2, rows, total), (2, 1, 0, 3))


LAG = 4
GROUPS = 4
SPACES = 8
PLANES = 4
BLOCK = 32
TOTAL = 128
SITES = 512
SPAN = 3 * SITES
QUADS = 4
CHUNK = 8
STEPS = TOTAL // 2 // CHUNK
CHUNK_ROWS = CHUNK * BLOCK
QUAD_ROWS = CHUNK * BLOCK // QUADS
WINDOW = BLOCK + TOTAL // 2
PART = WINDOW // QUADS


def ring(position):
    return position + lax.div(position, 2) * (1 - 2 * lax.rem(position, 2))


def fast_kernel(
    slots_ref,
    momentum_ref,
    block_ref,
    out_ref,
    gathered,
    swapped,
    wide,
    turned,
    placed,
    weighted,
    part,
    pair_out,
    part_in,
    sums,
    rounded,
    rounded_in,
    total,
    swap_out,
    swap_one,
    swap_two,
    extended,
    assembled,
    local_sem,
    gather_send,
    gather_recv,
    pair_send,
    pair_recv,
    sum_send,
    sum_recv,
    one_send,
    one_recv,
    two_send,
    two_recv,
):
    scale = jnp.float32(1.0 / math.sqrt(SITES * SPACES))
    group = lax.axis_index("group")
    space = lax.axis_index("space")
    core = lax.rem(space, 2)
    plane = lax.div(space, 2)
    position = ring(group)

    barrier = pltpu.get_barrier_semaphore()
    for off in range(1, GROUPS):
        pl.semaphore_signal(
            barrier, inc=1, device_id={"group": lax.rem(group + off, GROUPS)}, device_id_type=MESH
        )
    for off in range(1, PLANES):
        pl.semaphore_signal(
            barrier,
            inc=1,
            device_id={"space": lax.rem(plane + off, PLANES) * 2 + core},
            device_id_type=MESH,
        )
    pl.semaphore_signal(
        barrier, inc=1, device_id={"space": plane * 2 + 1 - core}, device_id_type=MESH
    )
    pl.semaphore_wait(barrier, GROUPS + PLANES - 1)

    def gather_copy(lane, target, source, owner, half):
        return pltpu.make_async_remote_copy(
            src_ref=source.at[half],
            dst_ref=gathered.at[half, owner],
            send_sem=gather_send.at[lane],
            recv_sem=gather_recv.at[lane],
            device_id={"group": target},
            device_id_type=MESH,
        )

    beside = group + 1 - 2 * lax.rem(group, 2)
    across = group + 2 - 4 * lax.div(group, 2)
    sends = [
        gather_copy(0, beside, block_ref, group, 0),
        gather_copy(1, across, block_ref, group, 1),
        gather_copy(2, beside, block_ref, group, 1),
        gather_copy(3, across, block_ref, group, 0),
    ]
    passed = [
        gather_copy(4, across, gathered.at[:, beside], beside, 0),
        gather_copy(5, beside, gathered.at[:, across], across, 1),
    ]
    for copy in sends:
        copy.start()
    own = pltpu.make_async_copy(block_ref, gathered.at[:, group], local_sem)
    own.start()
    for copy, onward in zip(sends, passed):
        copy.wait_recv()
        onward.start()

    sites = space * SITES + lax.broadcasted_iota(jnp.int32, (8, SITES), 1)
    coord_x = sites & (L - 1)
    coord_y = (sites >> 6) & (L - 1)
    coord_z = sites >> 12
    phase = momentum_ref[0] * coord_x + momentum_ref[1] * coord_y + momentum_ref[2] * coord_z
    angle = (phase & (L - 1)).astype(jnp.float32) * jnp.float32(2.0 * math.pi / L)
    cosine = jnp.cos(angle)
    sine = jnp.sin(angle)

    for x in range(TOTAL):
        slot = ring(lax.rem(position + x // BLOCK, GROUPS)) * BLOCK + x % BLOCK
        value = jnp.full((1, LANES), slots_ref[slot], jnp.int32)
        placed[x : x + 1, :] = value
        placed[TOTAL + x : TOTAL + x + 1, :] = value

    lane = lax.broadcasted_iota(jnp.int32, (PART, 2 * TOTAL), 1)
    lane_half = lane // TOTAL
    lane_group = (lane // BLOCK) % GROUPS
    lane_part = (lane // 16) % 2
    lane_vector = (2 * lane_group + lane_half) * 16 + lane % 16
    picks = []
    for c in range(2):
        for q in range(QUADS):
            wanted = placed[pl.ds(q, PART, stride=QUADS), :]
            wanted = jnp.concatenate([wanted, wanted], axis=1)
            hit = jnp.logical_and(lane_vector == wanted, lane_part == c)
            picks.append(jnp.where(hit, 1.0, 0.0).astype(jnp.float32))
    pick = jnp.concatenate(picks, axis=0).astype(jnp.bfloat16)

    own.wait()
    for copy in sends[:2]:
        copy.wait_send()
    for copy in sends[2:] + passed:
        copy.wait()

    swapped[:, :, :16, :] = -gathered[:, :, 16:, :]
    swapped[:, :, 16:, :] = gathered[:, :, :16, :]

    for a in range(3):
        rows = gathered[:, :, :, a * SITES : (a + 1) * SITES].reshape(2 * TOTAL, SITES)
        table = jnp.dot(pick, rows, preferred_element_type=jnp.float32)
        for c in range(2):
            for q in range(QUADS):
                first = (c * QUADS + q) * PART
                for s in range(SITES // LANES):
                    wide[c * 3 + a, s, q] = table[first : first + PART, s * LANES : (s + 1) * LANES]
    for s in range(SITES // LANES):
        cos_s = cosine[:, s * LANES : (s + 1) * LANES]
        sin_s = sine[:, s * LANES : (s + 1) * LANES]
        for q in range(QUADS):
            for a in range(3):
                re = wide[a, s, q, 0:8]
                im = wide[3 + a, s, q, 0:8]
                turned[a, s, q] = re * cos_s - im * sin_s
                turned[3 + a, s, q] = re * sin_s + im * cos_s

    def fill(step):
        def chunk(s, carry):
            for q in range(QUADS):
                tr = [turned[a, s, q] for a in range(3)]
                ti = [turned[3 + a, s, q] for a in range(3)]
                for pair in range(CHUNK // 2):
                    crosses = []
                    for k in range(2):
                        on = q + 1 + 2 * pair + k
                        at = pl.ds((CHUNK // QUADS) * step + on // QUADS, 8)
                        re = [wide[a, s, on % QUADS, at] for a in range(3)]
                        im = [wide[3 + a, s, on % QUADS, at] for a in range(3)]
                        made = []
                        for a in range(3):
                            b, c = (a + 1) % 3, (a + 2) % 3
                            made.append(
                                (re[b] * tr[c] - im[b] * ti[c]) - (re[c] * tr[b] - im[c] * ti[b])
                            )
                            made.append(
                                (re[b] * ti[c] + im[b] * tr[c]) - (re[c] * ti[b] + im[c] * tr[b])
                            )
                        crosses.append(made)
                    top = q * QUAD_ROWS + pair * 16
                    for a in range(3):
                        for c in range(2):
                            both = jnp.concatenate([crosses[k][2 * a + c] for k in range(2)], axis=0)
                            base = pl.multiple_of(c * SPAN + a * SITES + s * LANES, LANES)
                            weighted[top : top + 16, pl.ds(base, LANES)] = both.astype(jnp.bfloat16)
            return carry

        lax.fori_loop(0, SITES // LANES, chunk, 0)

    def pair_copy(step):
        return pltpu.make_async_remote_copy(
            src_ref=pair_out.at[step],
            dst_ref=part_in.at[step],
            send_sem=pair_send.at[step],
            recv_sem=pair_recv.at[step],
            device_id={"space": plane * 2 + 1 - core},
            device_id_type=MESH,
        )

    def sum_copy(step, off):
        target = lax.rem(plane + off, PLANES)
        return pltpu.make_async_remote_copy(
            src_ref=rounded.at[step, target],
            dst_ref=rounded_in.at[off - 1, step],
            send_sem=sum_send.at[off - 1, step],
            recv_sem=sum_recv.at[off - 1, step],
            device_id={"space": target * 2 + core},
            device_id_type=MESH,
        )

    def one_copy(step):
        return pltpu.make_async_remote_copy(
            src_ref=swap_out.at[step],
            dst_ref=swap_one.at[step],
            send_sem=one_send.at[step],
            recv_sem=one_recv.at[step],
            device_id={"group": ring(lax.rem(position + 1, GROUPS))},
            device_id_type=MESH,
        )

    def two_copy(step):
        return pltpu.make_async_remote_copy(
            src_ref=swap_out.at[step],
            dst_ref=swap_two.at[step - STEPS // 2],
            send_sem=two_send.at[step - STEPS // 2],
            recv_sem=two_recv.at[step - STEPS // 2],
            device_id={"group": ring(lax.rem(position + 2, GROUPS))},
            device_id_type=MESH,
        )

    def quad_of(shape):
        return lax.broadcasted_iota(jnp.int32, shape, len(shape) - 1) // 32

    def forward(step):
        pair_copy(step).wait()
        quad = quad_of((QUAD_ROWS, LANES))
        mine = []
        for q in range(QUADS):
            at = slice(q * QUAD_ROWS, (q + 1) * QUAD_ROWS)
            mine.append(part[step, core, at] + part_in[step, at].astype(jnp.float32))
        for t in range(PLANES):
            value = None
            for q in range(QUADS):
                shift = 32 * (q - t) % LANES
                moved = pltpu.roll(mine[q], shift, 1) if shift else mine[q]
                value = moved if value is None else jnp.where(quad == q, moved, value)
            sums[t] = value
            rounded[step, t] = value.astype(jnp.bfloat16)
        for off in range(1, PLANES):
            sum_copy(step, off).start()
        total[step] = sums[plane]

    def finish(step):
        value = total[step]
        for off in range(1, PLANES):
            sum_copy(step, off).wait()
            value = value + rounded_in[off - 1, step].astype(jnp.float32)
        swap_out[step] = value.astype(jnp.bfloat16)
        one_copy(step).start()

        @pl.when(step >= STEPS // 2)
        def _():
            two_copy(step).start()

        extended[pl.ds(step * CHUNK, CHUNK), 16:24] = value.reshape(CHUNK, 8, LANES)

    def body(step, carry):
        fill(step)

        @pl.when(step >= 1)
        def _():
            forward(step - 1)

        dims = (((1,), (1,)), ((), ()))
        product = lax.dot_general(
            weighted[:, :SPAN],
            gathered[...].reshape(2 * TOTAL, SPAN),
            dims,
            preferred_element_type=jnp.float32,
        ) + lax.dot_general(
            weighted[:, SPAN:],
            swapped[...].reshape(2 * TOTAL, SPAN),
            dims,
            preferred_element_type=jnp.float32,
        )
        part[step, 0] = product[:, :LANES]
        part[step, 1] = product[:, LANES:]
        pair_out[step] = part[step, 1 - core].astype(jnp.bfloat16)
        pair_copy(step).start()

        @pl.when(step >= LAG)
        def _():
            finish(step - LAG)

        return carry

    lax.fori_loop(0, STEPS, body, 0)
    forward(STEPS - 1)
    for step in range(STEPS - LAG, STEPS):
        finish(step)

    for step in range(STEPS):
        at = slice(step * CHUNK, (step + 1) * CHUNK)
        one_copy(step).wait()
        extended[at, 8:16] = swap_one[step].astype(jnp.float32).reshape(CHUNK, 8, LANES)
        if step >= STEPS // 2:
            two_copy(step).wait()
            extended[at, 0:8] = (
                swap_two[step - STEPS // 2].astype(jnp.float32).reshape(CHUNK, 8, LANES)
            )

    quad = quad_of((8, LANES))

    def at_distance(d):
        if d > 0:
            return extended[d - 1, 16:24]
        if d == 0:
            return jnp.zeros((8, LANES), jnp.float32)
        row, rest = divmod(TOTAL // 2 + d, QUADS)
        value = extended[-d - 1, row : row + 8]
        if rest:
            later = extended[-d - 1, row + 1 : row + 9]
            value = pltpu.roll(jnp.where(quad >= rest, value, later), LANES - 32 * rest, 1)
        return -value

    def wrapped(d):
        return d - TOTAL if d > TOTAL // 2 else d

    recent = [at_distance(d) for d in range(-TOTAL // 2 + 1, -TOTAL // 2 + 4)]
    for e in range(-TOTAL // 2 + 4, TOTAL // 2 + 4):
        recent.append(at_distance(wrapped(e)))
        value = recent[-1]
        for q in range(1, QUADS):
            value = jnp.where(quad == q, recent[-1 - q], value)
        row = e % TOTAL
        assembled[row * 8 : row * 8 + 8, :] = value

    columns = lax.broadcasted_iota(jnp.int32, (TOTAL, TOTAL), 1)
    for row in range(8):
        piece = assembled[pl.ds(row, TOTAL, stride=8), :].T
        high = piece.astype(jnp.bfloat16)
        low = (piece - high.astype(jnp.float32)).astype(jnp.bfloat16)
        spot = jnp.where(placed[QUADS * row : QUADS * row + TOTAL, :] == columns, 1.0, 0.0)
        spot = spot.astype(jnp.bfloat16)
        moved = jnp.dot(
            jnp.concatenate([high, low], axis=1),
            jnp.concatenate([spot, spot], axis=0),
            preferred_element_type=jnp.float32,
        )
        out_ref[QUADS * row : QUADS * row + QUADS] = (moved * scale).reshape(QUADS, 32, TOTAL)


def fast(vectors, momentum, assignment):
    mine = jnp.transpose(vectors.reshape(2, 16, 2, 3, SITES), (0, 2, 1, 3, 4)).reshape(2, BLOCK, SPAN)
    dma = pltpu.SemaphoreType.DMA
    f32, b16 = jnp.float32, jnp.bfloat16
    out = pl.pallas_call(
        fast_kernel,
        out_shape=jax.ShapeDtypeStruct((BLOCK, 32, TOTAL), f32),
        in_specs=[
            pl.BlockSpec(memory_space=pltpu.SMEM),
            pl.BlockSpec(memory_space=pltpu.SMEM),
            pl.BlockSpec(memory_space=pltpu.VMEM),
        ],
        out_specs=pl.BlockSpec(memory_space=pltpu.VMEM),
        scratch_shapes=[
            pltpu.VMEM((2, GROUPS, BLOCK, SPAN), b16),
            pltpu.VMEM((2, GROUPS, BLOCK, SPAN), b16),
            pltpu.VMEM((6, SITES // LANES, QUADS, PART, LANES), f32),
            pltpu.VMEM((6, SITES // LANES, QUADS, 8, LANES), f32),
            pltpu.VMEM((2 * TOTAL, LANES), jnp.int32),
            pltpu.VMEM((CHUNK_ROWS, 2 * SPAN), b16),
            pltpu.VMEM((STEPS, 2, CHUNK_ROWS, LANES), f32),
            pltpu.VMEM((STEPS, CHUNK_ROWS, LANES), b16),
            pltpu.VMEM((STEPS, CHUNK_ROWS, LANES), b16),
            pltpu.VMEM((PLANES, QUAD_ROWS, LANES), f32),
            pltpu.VMEM((STEPS, PLANES, QUAD_ROWS, LANES), b16),
            pltpu.VMEM((PLANES - 1, STEPS, QUAD_ROWS, LANES), b16),
            pltpu.VMEM((STEPS, QUAD_ROWS, LANES), f32),
            pltpu.VMEM((STEPS, QUAD_ROWS, LANES), b16),
            pltpu.VMEM((STEPS, QUAD_ROWS, LANES), b16),
            pltpu.VMEM((STEPS // 2, QUAD_ROWS, LANES), b16),
            pltpu.VMEM((TOTAL // 2, 24, LANES), f32),
            pltpu.VMEM((8 * TOTAL, LANES), f32),
            dma,
            dma((6,)),
            dma((6,)),
            dma((STEPS,)),
            dma((STEPS,)),
            dma((PLANES - 1, STEPS)),
            dma((PLANES - 1, STEPS)),
            dma((STEPS,)),
            dma((STEPS,)),
            dma((STEPS // 2,)),
            dma((STEPS // 2,)),
        ],
        compiler_params=pltpu.CompilerParams(
            collective_id=0, has_side_effects=True, vmem_limit_bytes=48 * 1024 * 1024
        ),
    )(assignment, momentum, mine)
    return jnp.transpose(out.reshape(BLOCK, 2, 16, TOTAL), (2, 1, 0, 3))


def local(groups, spaces, vectors, momentum, assignment):
    if (groups, spaces) == (GROUPS, SPACES) and vectors.shape == (BLOCK, 2, 3, SITES):
        return fast(vectors, momentum, assignment)
    return general(groups, spaces, vectors, momentum, assignment)


def solution(mesh):
    return jax.shard_map(
        functools.partial(local, mesh.shape["group"], mesh.shape["space"]),
        mesh=mesh,
        in_specs=(P("group", None, None, "space"), P(), P()),
        out_specs=P("space", None, "group", None),
        check_vma=False,
    )
```

```python
import functools
import math

import jax
import jax.numpy as jnp
from jax import lax
from jax.experimental import pallas as pl
from jax.experimental.pallas import tpu as pltpu
from jax.sharding import PartitionSpec as P

L = 64
MESH = pl.DeviceIdType.MESH
LANES = 128
ROWS = 16
SLOTS = 4


def general_kernel(
    groups,
    spaces,
    slots_ref,
    momentum_ref,
    block_ref,
    out_ref,
    gathered,
    wide,
    right,
    weighted,
    part,
    pair_out,
    part_in,
    rounded,
    rounded_in,
    local_sem,
    gather_send,
    gather_recv,
    pair_send,
    pair_recv,
    sum_send,
    sum_recv,
):
    block = block_ref.shape[1]
    site_count = block_ref.shape[2]
    total = groups * block
    rows = total // spaces
    planes = spaces // 2
    steps = block // SLOTS
    span = 3 * site_count
    scale = jnp.float32(1.0 / math.sqrt(site_count * spaces))
    group = lax.axis_index("group")
    space = lax.axis_index("space")
    core = lax.rem(space, 2)
    plane = lax.div(space, 2)

    barrier = pltpu.get_barrier_semaphore()
    for off in range(1, groups):
        pl.semaphore_signal(
            barrier, inc=1, device_id={"group": lax.rem(group + off, groups)}, device_id_type=MESH
        )
    for off in range(1, planes):
        pl.semaphore_signal(
            barrier,
            inc=1,
            device_id={"space": lax.rem(plane + off, planes) * 2 + core},
            device_id_type=MESH,
        )
    pl.semaphore_signal(
        barrier, inc=1, device_id={"space": plane * 2 + 1 - core}, device_id_type=MESH
    )
    pl.semaphore_wait(barrier, groups + planes - 1)

    def gather_copy(lane, target, source, owner, first, count):
        at = pl.ds(first, count)
        return pltpu.make_async_remote_copy(
            src_ref=source.at[at],
            dst_ref=gathered.at[owner, at],
            send_sem=gather_send.at[lane],
            recv_sem=gather_recv.at[lane],
            device_id={"group": target},
            device_id_type=MESH,
        )

    square = groups == 4
    if square:
        beside = group + 1 - 2 * lax.rem(group, 2)
        across = group + 2 - 4 * lax.div(group, 2)
        sends = [
            gather_copy(0, beside, block_ref, group, 0, 3),
            gather_copy(1, across, block_ref, group, 3, 3),
            gather_copy(2, beside, block_ref, group, 3, 3),
            gather_copy(3, across, block_ref, group, 0, 3),
        ]
        passed = [
            gather_copy(4, across, gathered.at[beside], beside, 0, 3),
            gather_copy(5, beside, gathered.at[across], across, 3, 3),
        ]
    else:
        sends = [
            gather_copy(off - 1, lax.rem(group + off, groups), block_ref, group, 0, 6)
            for off in range(1, groups)
        ]
    for copy in sends:
        copy.start()
    own = pltpu.make_async_copy(block_ref, gathered.at[group], local_sem)
    own.start()
    if square:
        for copy, onward in zip(sends, passed):
            copy.wait_recv()
            onward.start()

    sites = space * site_count + lax.broadcasted_iota(jnp.int32, (8, site_count), 1)
    coord_x = sites & (L - 1)
    coord_y = (sites >> 6) & (L - 1)
    coord_z = sites >> 12
    phase = momentum_ref[0] * coord_x + momentum_ref[1] * coord_y + momentum_ref[2] * coord_z
    angle = (phase & (L - 1)).astype(jnp.float32) * jnp.float32(2.0 * math.pi / L)
    cosine = jnp.cos(angle)[0:1]
    sine = jnp.sin(angle)[0:1]

    own.wait()
    if square:
        for copy in sends[:2]:
            copy.wait_send()
        for copy in sends[2:] + passed:
            copy.wait()
    else:
        for copy in sends:
            copy.wait()

    for q in range(groups):
        for c in range(6):
            wide[c, q * block : (q + 1) * block, :] = gathered[q, c].astype(jnp.float32)

    for a in range(3):
        real = wide[a].T.astype(jnp.bfloat16)
        imag = wide[3 + a].T.astype(jnp.bfloat16)
        low, high = a * site_count, (a + 1) * site_count
        right[low:high, :total] = real
        right[low:high, total:] = imag
        right[span + low : span + high, :total] = -imag
        right[span + low : span + high, total:] = real

    def fill(step, first, stop):
        def one(half, carry):
            k = slots_ref[group * block + SLOTS * step + half]
            row = [wide[c, pl.ds(k, 1), :] for c in range(6)]
            turn_re = [row[a] * cosine - row[3 + a] * sine for a in range(3)]
            turn_im = [row[a] * sine + row[3 + a] * cosine for a in range(3)]

            def tile(j, inner):
                top = pl.multiple_of(j * ROWS, ROWS)
                for s in range(0, site_count, LANES):
                    cols = slice(s, s + LANES)
                    re = [wide[a, pl.ds(top, ROWS), cols] for a in range(3)]
                    im = [wide[3 + a, pl.ds(top, ROWS), cols] for a in range(3)]
                    tr = [x[:, cols] for x in turn_re]
                    ti = [x[:, cols] for x in turn_im]
                    for a in range(3):
                        b, c = (a + 1) % 3, (a + 2) % 3
                        out_re = (re[b] * tr[c] - im[b] * ti[c]) - (re[c] * tr[b] - im[c] * ti[b])
                        out_im = (re[b] * ti[c] + im[b] * tr[c]) - (re[c] * ti[b] + im[c] * tr[b])
                        base = a * site_count + s
                        at = pl.ds(pl.multiple_of(half * total + top, ROWS), ROWS)
                        weighted[at, base : base + LANES] = out_re.astype(jnp.bfloat16)
                        weighted[at, span + base : span + base + LANES] = out_im.astype(jnp.bfloat16)
                return inner

            return lax.fori_loop(0, total // ROWS, tile, carry, unroll=True)

        lax.fori_loop(first, stop, one, 0)

    def pair_copy(step):
        return pltpu.make_async_remote_copy(
            src_ref=pair_out.at[step],
            dst_ref=part_in.at[step],
            send_sem=pair_send.at[step],
            recv_sem=pair_recv.at[step],
            device_id={"space": plane * 2 + 1 - core},
            device_id_type=MESH,
        )

    def sum_copy(step, off):
        target = lax.rem(plane + off, planes)
        return pltpu.make_async_remote_copy(
            src_ref=rounded.at[step, target],
            dst_ref=rounded_in.at[off - 1, step],
            send_sem=sum_send.at[off - 1, step],
            recv_sem=sum_recv.at[off - 1, step],
            device_id={"space": target * 2 + core},
            device_id_type=MESH,
        )

    def forward(step):
        pair_copy(step).wait()
        rounded[step] = (part[step, core] + part_in[step].astype(jnp.float32)).astype(jnp.bfloat16)
        for off in range(1, planes):
            sum_copy(step, off).start()
        out_ref[pl.ds(SLOTS * step, SLOTS)] = part[step, core, plane] + part_in[step, plane].astype(jnp.float32)

    def body(step, carry):
        fill(step, 0, SLOTS - 1)

        @pl.when(step >= 1)
        def _():
            forward(step - 1)

        fill(step, SLOTS - 1, SLOTS)
        product = jnp.dot(weighted[...], right[...], preferred_element_type=jnp.float32)
        for half in range(SLOTS):
            piece = product[half * total : (half + 1) * total].T
            for c in range(2):
                for i in range(spaces):
                    first = c * total + i * rows
                    part[step, i % 2, i // 2, half, c * rows : (c + 1) * rows] = piece[
                        first : first + rows
                    ]
        pair_out[step] = part[step, 1 - core].astype(jnp.bfloat16)
        pair_copy(step).start()

        return carry

    lax.fori_loop(0, steps, body, 0)
    forward(steps - 1)

    def finish(step, carry):
        value = out_ref[pl.ds(SLOTS * step, SLOTS)]
        for off in range(1, planes):
            sum_copy(step, off).wait()
            value = value + rounded_in[off - 1, step].astype(jnp.float32)
        out_ref[pl.ds(SLOTS * step, SLOTS)] = value * scale
        return carry

    lax.fori_loop(0, steps, finish, 0)


def general(groups, spaces, vectors, momentum, assignment):
    block, _, _, site_count = vectors.shape
    total = block * groups
    rows = total // spaces
    planes = spaces // 2
    steps = block // SLOTS
    mine = jnp.transpose(vectors, (1, 2, 0, 3)).reshape(6, block, site_count)
    dma = pltpu.SemaphoreType.DMA
    out = pl.pallas_call(
        functools.partial(general_kernel, groups, spaces),
        out_shape=jax.ShapeDtypeStruct((block, 2 * rows, total), jnp.float32),
        in_specs=[
            pl.BlockSpec(memory_space=pltpu.SMEM),
            pl.BlockSpec(memory_space=pltpu.SMEM),
            pl.BlockSpec(memory_space=pltpu.VMEM),
        ],
        out_specs=pl.BlockSpec(memory_space=pltpu.VMEM),
        scratch_shapes=[
            pltpu.VMEM((groups, 6, block, site_count), jnp.bfloat16),
            pltpu.VMEM((6, total, site_count), jnp.float32),
            pltpu.VMEM((6 * site_count, 2 * total), jnp.bfloat16),
            pltpu.VMEM((SLOTS * total, 6 * site_count), jnp.bfloat16),
            pltpu.VMEM((steps, 2, planes, SLOTS, 2 * rows, total), jnp.float32),
            pltpu.VMEM((steps, planes, SLOTS, 2 * rows, total), jnp.bfloat16),
            pltpu.VMEM((steps, planes, SLOTS, 2 * rows, total), jnp.bfloat16),
            pltpu.VMEM((steps, planes, SLOTS, 2 * rows, total), jnp.bfloat16),
            pltpu.VMEM((planes - 1, steps, SLOTS, 2 * rows, total), jnp.bfloat16),
            dma,
            dma((max(groups - 1, 6),)),
            dma((max(groups - 1, 6),)),
            dma((steps,)),
            dma((steps,)),
            dma((planes - 1, steps)),
            dma((planes - 1, steps)),
        ],
        compiler_params=pltpu.CompilerParams(
            collective_id=0, has_side_effects=True, vmem_limit_bytes=48 * 1024 * 1024
        ),
    )(assignment, momentum, mine)
    return jnp.transpose(out.reshape(block, 2, rows, total), (2, 1, 0, 3))


GROUPS = 4
SPACES = 8
PLANES = 4
BLOCK = 32
TOTAL = 128
SITES = 512
SPAN = 3 * SITES
QUADS = 4
CHUNK = 8
LAG = 4
TILES = SITES // LANES
SLICE = 3 * LANES
STEPS = TOTAL // 2 // CHUNK
CHUNK_ROWS = CHUNK * BLOCK
QUAD_ROWS = CHUNK * BLOCK // QUADS
WINDOW = BLOCK + TOTAL // 2
PART = WINDOW // QUADS
DISTANCES = TOTAL // 2


def ring(position):
    return position + lax.div(position, 2) * (1 - 2 * lax.rem(position, 2))


def fast_kernel(
    slots_any,
    momentum_any,
    block_any,
    out_ref,
    slots_ref,
    momentum_ref,
    block_ref,
    mine,
    gathered,
    wide,
    turned,
    turns,
    pick,
    in_order,
    placed,
    weighted,
    part,
    pair_out,
    part_in,
    sums,
    rounded,
    rounded_in,
    swap_out,
    swap_one,
    swap_two,
    extended,
    assembled,
    local_sem,
    own_sem,
    known_sem,
    gather_send,
    gather_recv,
    pair_send,
    pair_recv,
    sum_send,
    sum_recv,
    swap_send,
    swap_recv,
):
    scale = jnp.float32(1.0 / math.sqrt(SITES * SPACES))
    group = lax.axis_index("group")
    space = lax.axis_index("space")
    core = lax.rem(space, 2)
    plane = lax.div(space, 2)
    position = ring(group)

    loads = [
        pltpu.make_async_copy(block_any, block_ref, local_sem.at[0]),
        pltpu.make_async_copy(slots_any, slots_ref, local_sem.at[1]),
        pltpu.make_async_copy(momentum_any, momentum_ref, local_sem.at[2]),
    ]
    for load in loads:
        load.start()

    barrier = pltpu.get_barrier_semaphore()
    beside = group + 1 - 2 * lax.rem(group, 2)
    across = group + 2 - 4 * lax.div(group, 2)
    partner = plane + 1 - 2 * lax.rem(plane, 2)
    mirror = PLANES - 1 - plane
    second = lax.rem(plane + 2, PLANES)
    middle = lax.div(plane + 1, 2) == 1

    def at_plane(target):
        return {"space": target * 2 + core}

    def greet(semaphore, device):
        pl.semaphore_signal(semaphore, inc=1, device_id=device, device_id_type=MESH)

    greet(barrier, {"space": plane * 2 + 1 - core})
    greet(barrier, {"group": beside})
    greet(barrier, {"group": across})
    greet(barrier, at_plane(partner))

    @pl.when(middle)
    def _():
        greet(barrier, at_plane(mirror))

    loads[0].wait()
    for tile in range(TILES):
        for k in range(4):
            for a in range(3):
                rows = block_ref[8 * k : 8 * k + 8, a, :, tile * LANES : (tile + 1) * LANES]
                first = (k % 2) * 16
                mine[tile, k // 2, first : first + 16, a * LANES : (a + 1) * LANES] = rows.reshape(
                    16, LANES
                )
    own = pltpu.make_async_copy(mine, gathered.at[:, :, group, :, :SLICE], own_sem)
    own.start()

    @pl.when(middle)
    def _():
        pl.semaphore_wait(barrier, 5)
        greet(known_sem, at_plane(mirror))

    @pl.when(jnp.logical_not(middle))
    def _():
        pl.semaphore_wait(barrier, 4)

    def gather_copy(tile, lane, target, source, half, owner):
        return pltpu.make_async_remote_copy(
            src_ref=source,
            dst_ref=gathered.at[tile, half, owner, :, :SLICE],
            send_sem=gather_send.at[tile, lane],
            recv_sem=gather_recv.at[tile, lane],
            device_id={"group": target},
            device_id_type=MESH,
        )

    def leading(tile):
        return [
            gather_copy(tile, 0, beside, mine.at[tile, 0], 0, group),
            gather_copy(tile, 1, across, mine.at[tile, 1], 1, group),
        ]

    def trailing(tile):
        return [
            gather_copy(tile, 2, beside, mine.at[tile, 1], 1, group),
            gather_copy(tile, 3, across, mine.at[tile, 0], 0, group),
        ]

    def onward(tile):
        return [
            gather_copy(tile, 4, across, gathered.at[tile, 0, beside, :, :SLICE], 0, beside),
            gather_copy(tile, 5, beside, gathered.at[tile, 1, across, :, :SLICE], 1, across),
        ]

    def pass_on(tile):
        for copy, further in zip(leading(tile), onward(tile)):
            copy.wait_recv()
            further.start()

    for tile in range(TILES - 1):
        for copy in leading(tile) + trailing(tile):
            copy.start()

    for load in loads[1:]:
        load.wait()
    sites = space * SITES + lax.broadcasted_iota(jnp.int32, (8, SITES), 1)
    coord_x = sites & (L - 1)
    coord_y = (sites >> 6) & (L - 1)
    coord_z = sites >> 12
    phase = momentum_ref[0] * coord_x + momentum_ref[1] * coord_y + momentum_ref[2] * coord_z
    angle = (phase & (L - 1)).astype(jnp.float32) * jnp.float32(2.0 * math.pi / L)
    cosine = jnp.cos(angle)
    sine = jnp.sin(angle)
    for tile in range(TILES):
        turns[0, tile] = cosine[:, tile * LANES : (tile + 1) * LANES]
        turns[1, tile] = sine[:, tile * LANES : (tile + 1) * LANES]

    in_order[...] = jnp.broadcast_to(slots_ref[...].astype(jnp.float32), (TOTAL, LANES)).T.astype(jnp.int32)
    for block in range(GROUPS):
        first = pl.multiple_of(ring(lax.rem(position + block, GROUPS)) * BLOCK, BLOCK)
        value = in_order[pl.ds(first, BLOCK), :]
        placed[block * BLOCK : (block + 1) * BLOCK, :] = value
        placed[TOTAL + block * BLOCK : TOTAL + (block + 1) * BLOCK, :] = value

    own.wait()
    pass_on(0)
    for copy in leading(TILES - 1) + trailing(TILES - 1):
        copy.start()
    lane = lax.broadcasted_iota(jnp.int32, (PART, 2 * TOTAL), 1)
    lane_vector = (2 * ((lane // BLOCK) % GROUPS) + lane // TOTAL) * 16 + (lane // 2) % 16
    picks = []
    for c in range(2):
        for q in range(QUADS):
            wanted = placed[pl.ds(q, PART, stride=QUADS), :]
            wanted = jnp.concatenate([wanted, wanted], axis=1)
            hit = jnp.logical_and(lane_vector == wanted, lane % 2 == c)
            picks.append(jnp.where(hit, 1.0, 0.0).astype(jnp.float32))
    row = lax.broadcasted_iota(jnp.int32, (2 * TOTAL, 2 * TOTAL), 0)
    column = lax.broadcasted_iota(jnp.int32, (2 * TOTAL, 2 * TOTAL), 1)
    other = row + 1 - 2 * (row % 2)
    sign = (2 * (row % 2) - 1).astype(jnp.float32)
    picks.append(jnp.where(column == other, sign, 0.0))
    pick[...] = jnp.concatenate(picks, axis=0).astype(jnp.bfloat16)

    pass_on(1)
    pass_on(2)

    def arrived(tile):
        for copy in trailing(tile) + onward(tile):
            copy.wait_recv()

    def prepare(tile):
        rows = gathered[tile, :, :, :, :SLICE].reshape(2 * TOTAL, SLICE)
        table = jnp.dot(pick[...], rows, preferred_element_type=jnp.float32)
        gathered[tile, :, :, :, SLICE:] = (
            table[2 * QUADS * PART :].astype(jnp.bfloat16).reshape(2, GROUPS, BLOCK, SLICE)
        )
        for q in range(QUADS):
            for a in range(3):
                first = q * PART
                at = slice(a * LANES, (a + 1) * LANES)
                re = table[first : first + PART, at]
                im = table[QUADS * PART + first : QUADS * PART + first + PART, at]
                wide[a, tile, q] = re
                wide[3 + a, tile, q] = im
                wide[6 + a, tile, q] = re + im
                re, im = re[:8], im[:8]
                turn_re = re * turns[0, tile] - im * turns[1, tile]
                turn_im = re * turns[1, tile] + im * turns[0, tile]
                turned[a, tile, q] = turn_re
                turned[3 + a, tile, q] = turn_im
                turned[6 + a, tile, q] = turn_re + turn_im

    def fill(step, tile, count, into):
        for q in range(QUADS):
            turn = [turned[c, tile, q] for c in range(9)]
            for pair in range(count // 2):
                crosses = []
                for k in range(2):
                    on = q + 1 + 2 * pair + k
                    at = pl.ds((count // QUADS) * step + on // QUADS, 8)
                    side = [wide[c, tile, on % QUADS, at] for c in range(9)]
                    made = []
                    for a in range(3):
                        b, c = (a + 1) % 3, (a + 2) % 3
                        re, im, both = (
                            side[n + b] * turn[n + c] - side[n + c] * turn[n + b] for n in (0, 3, 6)
                        )
                        made += [re - im, both - (re + im)]
                    crosses.append(made)
                top = (q * count // 2 + pair) * 16
                for a in range(3):
                    for c in range(2):
                        both = jnp.concatenate([crosses[k][2 * a + c] for k in range(2)], axis=0)
                        base = (c * 3 + a) * LANES
                        into[top : top + 16, base : base + LANES] = both.astype(jnp.bfloat16)

    def times(values, tile):
        return lax.dot_general(
            values,
            gathered[tile].reshape(2 * TOTAL, 2 * SLICE),
            (((1,), (1,)), ((), ())),
            preferred_element_type=jnp.float32,
        )

    def early(step, carry):
        fill(STEPS - 1 - step, 0, CHUNK, weighted.at[0])
        value = times(weighted[0], 0)
        for h in range(2):
            part[step, h] = value[:, h * LANES : (h + 1) * LANES]

        @pl.when(step == 0)
        def _():
            pass_on(TILES - 1)

        return carry

    arrived(0)
    prepare(0)
    lax.fori_loop(0, STEPS, early, 0)
    for tile in range(1, TILES):
        arrived(tile)
        prepare(tile)
    for tile in range(TILES):
        for copy in leading(tile) + trailing(tile) + onward(tile):
            copy.wait_send()

    @pl.when(middle)
    def _():
        pl.semaphore_wait(known_sem, 1)
        greet(known_sem, at_plane(partner))

    @pl.when(jnp.logical_not(middle))
    def _():
        pl.semaphore_wait(known_sem, 1)

    def pair_copy(step):
        return pltpu.make_async_remote_copy(
            src_ref=pair_out.at[step],
            dst_ref=part_in.at[step],
            send_sem=pair_send.at[step],
            recv_sem=pair_recv.at[step],
            device_id={"space": plane * 2 + 1 - core},
            device_id_type=MESH,
        )

    def sum_copy(step, lane, source, slot, target):
        return pltpu.make_async_remote_copy(
            src_ref=source,
            dst_ref=rounded_in.at[slot, step],
            send_sem=sum_send.at[lane, step],
            recv_sem=sum_recv.at[slot, step],
            device_id=at_plane(target),
            device_id_type=MESH,
        )

    def onto(step):
        return [
            sum_copy(step, n, rounded.at[step, target], n, target)
            for n, target in enumerate((mirror, second, partner))
        ]

    def swap_copy(chunk, rows, reach):
        rows = pl.ds(rows.start, rows.stop - rows.start)
        return pltpu.make_async_remote_copy(
            src_ref=swap_out.at[chunk, rows],
            dst_ref=(swap_one if reach == 1 else swap_two).at[chunk, rows],
            send_sem=swap_send.at[reach - 1, chunk],
            recv_sem=swap_recv.at[reach - 1, chunk],
            device_id={"group": ring(lax.rem(position + reach, GROUPS))},
            device_id_type=MESH,
        )

    def quad_of(shape):
        return lax.broadcasted_iota(jnp.int32, shape, len(shape) - 1) // 32

    def forward(step):
        pair_copy(step).wait()
        quad = quad_of((QUAD_ROWS, LANES))
        held = []
        for q in range(QUADS):
            at = slice(q * QUAD_ROWS, (q + 1) * QUAD_ROWS)
            held.append(part[step, core, at] + part_in[step, at].astype(jnp.float32))
        for shift in (64, 32):
            low = (quad * 32 // shift) % 2 == 0
            apart = shift // 32
            for q in range(QUADS):
                if (q // apart) % 2 == 0:
                    one, two = held[q], held[q + apart]
                    held[q] = jnp.where(low, one, pltpu.roll(two, shift, 1))
                    held[q + apart] = jnp.where(low, pltpu.roll(one, LANES - shift, 1), two)
        for t in range(PLANES):
            sums[step, t] = held[t]
            rounded[step, t] = held[t].astype(jnp.bfloat16)
        for copy in onto(step):
            copy.start()

    half_rows = QUAD_ROWS // 2
    low_rows, high_rows = slice(0, half_rows), slice(half_rows, QUAD_ROWS)
    all_rows = slice(0, QUAD_ROWS)

    def reaches(chunk):
        one = high_rows if chunk < 2 else all_rows if chunk < 6 else low_rows
        two = None if chunk < 4 else high_rows if chunk < 6 else all_rows
        return one, two

    def finish(step):
        chunk = STEPS - 1 - step
        value = sums[step, plane]
        for n, copy in enumerate(onto(step)):
            copy.wait_recv()
            value = value + rounded_in[n, step].astype(jnp.float32)
        first = 16 * DISTANCES + chunk * CHUNK
        for k in range(CHUNK):
            extended[pl.ds(first + k, 8, stride=DISTANCES), :] = value[8 * k : 8 * k + 8]
        for k in range(0, 8, 2):
            both = [
                extended[pl.ds(pl.multiple_of(first + n * DISTANCES, CHUNK), CHUNK), :]
                for n in (k, k + 1)
            ]
            swap_out[chunk, 8 * k : 8 * k + 16] = jnp.concatenate(both, axis=0).astype(jnp.bfloat16)

        for low, high in ((0, 2), (2, 4), (4, 6), (6, 8)):

            @pl.when(jnp.logical_and(chunk >= low, chunk < high))
            def _():
                one, two = reaches(low)
                swap_copy(chunk, one, 1).start()
                if two is not None:
                    swap_copy(chunk, two, 2).start()

    def body(step, carry):
        def one(n, inner):
            fill(STEPS - 1 - step, 1 + n, CHUNK, weighted.at[n])
            return inner

        lax.fori_loop(0, TILES - 1, one, 0)
        value = times(weighted[0], 1)
        for n in range(1, TILES - 1):
            value = value + times(weighted[n], 1 + n)
        for h in range(2):
            part[step, h] += value[:, h * LANES : (h + 1) * LANES]
        pair_out[step] = part[step, 1 - core].astype(jnp.bfloat16)
        pair_copy(step).start()

        @pl.when(step >= 1)
        def _():
            forward(step - 1)

        @pl.when(step >= LAG)
        def _():
            finish(step - LAG)

        return carry

    lax.fori_loop(0, STEPS, body, 0)
    forward(STEPS - 1)

    def last(step, carry):
        finish(step)
        return carry

    lax.fori_loop(STEPS - LAG, STEPS, last, 0)
    for step in range(STEPS):
        for copy in onto(step):
            copy.wait_send()

    for chunk in reversed(range(STEPS)):
        for reach, rows in enumerate(reaches(chunk), 1):
            if rows is None:
                continue
            swap_copy(chunk, rows, reach).wait()
            came = (swap_one if reach == 1 else swap_two)[chunk, rows].astype(jnp.float32)
            for n in range((rows.stop - rows.start) // 8):
                row = (2 - reach) * 8 + rows.start // 8 + n
                first = row * DISTANCES + chunk * CHUNK
                extended[first : first + CHUNK, :] = came[8 * n : 8 * n + 8]

    quad = quad_of((8, LANES))

    def at_distance(d):
        if d > 0:
            return extended[pl.ds(16 * DISTANCES + d - 1, 8, stride=DISTANCES), :]
        if d == 0:
            return jnp.zeros((8, LANES), jnp.float32)
        row, rest = divmod(TOTAL // 2 + d, QUADS)
        value = extended[pl.ds(row * DISTANCES - d - 1, 8, stride=DISTANCES), :]
        if rest:
            later = extended[pl.ds((row + 1) * DISTANCES - d - 1, 8, stride=DISTANCES), :]
            value = pltpu.roll(jnp.where(quad >= rest, value, later), LANES - 32 * rest, 1)
        return -value

    def wrapped(d):
        return d - TOTAL if d > TOTAL // 2 else d

    recent = [at_distance(d) for d in range(-TOTAL // 2 + 1, -TOTAL // 2 + 4)]
    for e in range(-TOTAL // 2 + 4, TOTAL // 2 + 4):
        recent.append(at_distance(wrapped(e)))
        value = recent[-1]
        for q in range(1, QUADS):
            value = jnp.where(quad == q, recent[-1 - q], value)
        row = e % TOTAL
        assembled[row * 8 : row * 8 + 8, :] = value

    columns = lax.broadcasted_iota(jnp.int32, (TOTAL, TOTAL), 1)
    for row in range(8):
        piece = assembled[pl.ds(row, TOTAL, stride=8), :].T
        high = piece.astype(jnp.bfloat16)
        low = (piece - high.astype(jnp.float32)).astype(jnp.bfloat16)
        spot = jnp.where(placed[QUADS * row : QUADS * row + TOTAL, :] == columns, 1.0, 0.0)
        spot = spot.astype(jnp.bfloat16)
        moved = jnp.dot(
            jnp.concatenate([high, low], axis=1),
            jnp.concatenate([spot, spot], axis=0),
            preferred_element_type=jnp.float32,
        )
        moved = moved * scale
        for q in range(QUADS):
            out_ref[pl.ds(QUADS * row + q, 32, stride=BLOCK), :] = moved[32 * q : 32 * q + 32]


def fast(vectors, momentum, assignment):
    mine = jnp.transpose(vectors, (0, 2, 1, 3))
    dma = pltpu.SemaphoreType.DMA
    f32, b16 = jnp.float32, jnp.bfloat16
    out = pl.pallas_call(
        fast_kernel,
        out_shape=jax.ShapeDtypeStruct((32 * BLOCK, TOTAL), f32),
        in_specs=[
            pl.BlockSpec(memory_space=pl.ANY),
            pl.BlockSpec(memory_space=pl.ANY),
            pl.BlockSpec(memory_space=pl.ANY),
        ],
        out_specs=pl.BlockSpec(memory_space=pltpu.VMEM),
        scratch_shapes=[
            pltpu.VMEM((1, TOTAL), jnp.int32),
            pltpu.SMEM((3,), jnp.int32),
            pltpu.VMEM((BLOCK, 3, 2, SITES), b16),
            pltpu.VMEM((TILES, 2, BLOCK, SLICE), b16),
            pltpu.VMEM((TILES, 2, GROUPS, BLOCK, 2 * SLICE), b16),
            pltpu.VMEM((9, TILES, QUADS, PART, LANES), f32),
            pltpu.VMEM((9, TILES, QUADS, 8, LANES), f32),
            pltpu.VMEM((2, TILES, 8, LANES), f32),
            pltpu.VMEM((2 * QUADS * PART + 2 * TOTAL, 2 * TOTAL), b16),
            pltpu.VMEM((TOTAL, LANES), jnp.int32),
            pltpu.VMEM((2 * TOTAL, LANES), jnp.int32),
            pltpu.VMEM((TILES - 1, CHUNK_ROWS, 2 * SLICE), b16),
            pltpu.VMEM((STEPS, 2, CHUNK_ROWS, LANES), f32),
            pltpu.VMEM((STEPS, CHUNK_ROWS, LANES), b16),
            pltpu.VMEM((STEPS, CHUNK_ROWS, LANES), b16),
            pltpu.VMEM((STEPS, PLANES, QUAD_ROWS, LANES), f32),
            pltpu.VMEM((STEPS, PLANES, QUAD_ROWS, LANES), b16),
            pltpu.VMEM((PLANES - 1, STEPS, QUAD_ROWS, LANES), b16),
            pltpu.VMEM((STEPS, QUAD_ROWS, LANES), b16),
            pltpu.VMEM((STEPS, QUAD_ROWS, LANES), b16),
            pltpu.VMEM((STEPS, QUAD_ROWS, LANES), b16),
            pltpu.VMEM((24 * DISTANCES, LANES), f32),
            pltpu.VMEM((8 * TOTAL, LANES), f32),
            dma((3,)),
            dma,
            pltpu.SemaphoreType.REGULAR,
            dma((TILES, 6)),
            dma((TILES, 6)),
            dma((STEPS,)),
            dma((STEPS,)),
            dma((PLANES - 1, STEPS)),
            dma((PLANES - 1, STEPS)),
            dma((2, STEPS)),
            dma((2, STEPS)),
        ],
        compiler_params=pltpu.CompilerParams(
            collective_id=0, has_side_effects=True, vmem_limit_bytes=48 * 1024 * 1024
        ),
    )(assignment.reshape(1, TOTAL), momentum, mine)
    return out.reshape(16, 2, BLOCK, TOTAL)


def local(groups, spaces, vectors, momentum, assignment):
    if (groups, spaces) == (GROUPS, SPACES) and vectors.shape == (BLOCK, 2, 3, SITES):
        return fast(vectors, momentum, assignment)
    return general(groups, spaces, vectors, momentum, assignment)


def solution(mesh):
    return jax.shard_map(
        functools.partial(local, mesh.shape["group"], mesh.shape["space"]),
        mesh=mesh,
        in_specs=(P("group", None, None, "space"), P(), P()),
        out_specs=P("space", None, "group", None),
        check_vma=False,
    )
```

```python
import functools
import math

import jax
import jax.numpy as jnp
from jax import lax
from jax.experimental import pallas as pl
from jax.experimental.pallas import tpu as pltpu
from jax.sharding import PartitionSpec as P

L = 64
MESH = pl.DeviceIdType.MESH
LANES = 128
ROWS = 16
SLOTS = 4


def general_kernel(
    groups,
    spaces,
    slots_ref,
    momentum_ref,
    block_ref,
    out_ref,
    gathered,
    wide,
    right,
    weighted,
    part,
    pair_out,
    part_in,
    rounded,
    rounded_in,
    local_sem,
    gather_send,
    gather_recv,
    pair_send,
    pair_recv,
    sum_send,
    sum_recv,
):
    block = block_ref.shape[1]
    site_count = block_ref.shape[2]
    total = groups * block
    rows = total // spaces
    planes = spaces // 2
    steps = block // SLOTS
    span = 3 * site_count
    scale = jnp.float32(1.0 / math.sqrt(site_count * spaces))
    group = lax.axis_index("group")
    space = lax.axis_index("space")
    core = lax.rem(space, 2)
    plane = lax.div(space, 2)

    barrier = pltpu.get_barrier_semaphore()
    for off in range(1, groups):
        pl.semaphore_signal(
            barrier, inc=1, device_id={"group": lax.rem(group + off, groups)}, device_id_type=MESH
        )
    for off in range(1, planes):
        pl.semaphore_signal(
            barrier,
            inc=1,
            device_id={"space": lax.rem(plane + off, planes) * 2 + core},
            device_id_type=MESH,
        )
    pl.semaphore_signal(
        barrier, inc=1, device_id={"space": plane * 2 + 1 - core}, device_id_type=MESH
    )
    pl.semaphore_wait(barrier, groups + planes - 1)

    def gather_copy(lane, target, source, owner, first, count):
        at = pl.ds(first, count)
        return pltpu.make_async_remote_copy(
            src_ref=source.at[at],
            dst_ref=gathered.at[owner, at],
            send_sem=gather_send.at[lane],
            recv_sem=gather_recv.at[lane],
            device_id={"group": target},
            device_id_type=MESH,
        )

    square = groups == 4
    if square:
        beside = group + 1 - 2 * lax.rem(group, 2)
        across = group + 2 - 4 * lax.div(group, 2)
        sends = [
            gather_copy(0, beside, block_ref, group, 0, 3),
            gather_copy(1, across, block_ref, group, 3, 3),
            gather_copy(2, beside, block_ref, group, 3, 3),
            gather_copy(3, across, block_ref, group, 0, 3),
        ]
        passed = [
            gather_copy(4, across, gathered.at[beside], beside, 0, 3),
            gather_copy(5, beside, gathered.at[across], across, 3, 3),
        ]
    else:
        sends = [
            gather_copy(off - 1, lax.rem(group + off, groups), block_ref, group, 0, 6)
            for off in range(1, groups)
        ]
    for copy in sends:
        copy.start()
    own = pltpu.make_async_copy(block_ref, gathered.at[group], local_sem)
    own.start()
    if square:
        for copy, onward in zip(sends, passed):
            copy.wait_recv()
            onward.start()

    sites = space * site_count + lax.broadcasted_iota(jnp.int32, (8, site_count), 1)
    coord_x = sites & (L - 1)
    coord_y = (sites >> 6) & (L - 1)
    coord_z = sites >> 12
    phase = momentum_ref[0] * coord_x + momentum_ref[1] * coord_y + momentum_ref[2] * coord_z
    angle = (phase & (L - 1)).astype(jnp.float32) * jnp.float32(2.0 * math.pi / L)
    cosine = jnp.cos(angle)[0:1]
    sine = jnp.sin(angle)[0:1]

    own.wait()
    if square:
        for copy in sends[:2]:
            copy.wait_send()
        for copy in sends[2:] + passed:
            copy.wait()
    else:
        for copy in sends:
            copy.wait()

    for q in range(groups):
        for c in range(6):
            wide[c, q * block : (q + 1) * block, :] = gathered[q, c].astype(jnp.float32)

    for a in range(3):
        real = wide[a].T.astype(jnp.bfloat16)
        imag = wide[3 + a].T.astype(jnp.bfloat16)
        low, high = a * site_count, (a + 1) * site_count
        right[low:high, :total] = real
        right[low:high, total:] = imag
        right[span + low : span + high, :total] = -imag
        right[span + low : span + high, total:] = real

    def fill(step, first, stop):
        def one(half, carry):
            k = slots_ref[group * block + SLOTS * step + half]
            row = [wide[c, pl.ds(k, 1), :] for c in range(6)]
            turn_re = [row[a] * cosine - row[3 + a] * sine for a in range(3)]
            turn_im = [row[a] * sine + row[3 + a] * cosine for a in range(3)]

            def tile(j, inner):
                top = pl.multiple_of(j * ROWS, ROWS)
                for s in range(0, site_count, LANES):
                    cols = slice(s, s + LANES)
                    re = [wide[a, pl.ds(top, ROWS), cols] for a in range(3)]
                    im = [wide[3 + a, pl.ds(top, ROWS), cols] for a in range(3)]
                    tr = [x[:, cols] for x in turn_re]
                    ti = [x[:, cols] for x in turn_im]
                    for a in range(3):
                        b, c = (a + 1) % 3, (a + 2) % 3
                        out_re = (re[b] * tr[c] - im[b] * ti[c]) - (re[c] * tr[b] - im[c] * ti[b])
                        out_im = (re[b] * ti[c] + im[b] * tr[c]) - (re[c] * ti[b] + im[c] * tr[b])
                        base = a * site_count + s
                        at = pl.ds(pl.multiple_of(half * total + top, ROWS), ROWS)
                        weighted[at, base : base + LANES] = out_re.astype(jnp.bfloat16)
                        weighted[at, span + base : span + base + LANES] = out_im.astype(jnp.bfloat16)
                return inner

            return lax.fori_loop(0, total // ROWS, tile, carry, unroll=True)

        lax.fori_loop(first, stop, one, 0)

    def pair_copy(step):
        return pltpu.make_async_remote_copy(
            src_ref=pair_out.at[step],
            dst_ref=part_in.at[step],
            send_sem=pair_send.at[step],
            recv_sem=pair_recv.at[step],
            device_id={"space": plane * 2 + 1 - core},
            device_id_type=MESH,
        )

    def sum_copy(step, off):
        target = lax.rem(plane + off, planes)
        return pltpu.make_async_remote_copy(
            src_ref=rounded.at[step, target],
            dst_ref=rounded_in.at[off - 1, step],
            send_sem=sum_send.at[off - 1, step],
            recv_sem=sum_recv.at[off - 1, step],
            device_id={"space": target * 2 + core},
            device_id_type=MESH,
        )

    def forward(step):
        pair_copy(step).wait()
        rounded[step] = (part[step, core] + part_in[step].astype(jnp.float32)).astype(jnp.bfloat16)
        for off in range(1, planes):
            sum_copy(step, off).start()
        out_ref[pl.ds(SLOTS * step, SLOTS)] = part[step, core, plane] + part_in[step, plane].astype(jnp.float32)

    def body(step, carry):
        fill(step, 0, SLOTS - 1)

        @pl.when(step >= 1)
        def _():
            forward(step - 1)

        fill(step, SLOTS - 1, SLOTS)
        product = jnp.dot(weighted[...], right[...], preferred_element_type=jnp.float32)
        for half in range(SLOTS):
            piece = product[half * total : (half + 1) * total].T
            for c in range(2):
                for i in range(spaces):
                    first = c * total + i * rows
                    part[step, i % 2, i // 2, half, c * rows : (c + 1) * rows] = piece[
                        first : first + rows
                    ]
        pair_out[step] = part[step, 1 - core].astype(jnp.bfloat16)
        pair_copy(step).start()

        return carry

    lax.fori_loop(0, steps, body, 0)
    forward(steps - 1)

    def finish(step, carry):
        value = out_ref[pl.ds(SLOTS * step, SLOTS)]
        for off in range(1, planes):
            sum_copy(step, off).wait()
            value = value + rounded_in[off - 1, step].astype(jnp.float32)
        out_ref[pl.ds(SLOTS * step, SLOTS)] = value * scale
        return carry

    lax.fori_loop(0, steps, finish, 0)


def general(groups, spaces, vectors, momentum, assignment):
    block, _, _, site_count = vectors.shape
    total = block * groups
    rows = total // spaces
    planes = spaces // 2
    steps = block // SLOTS
    mine = jnp.transpose(vectors, (1, 2, 0, 3)).reshape(6, block, site_count)
    dma = pltpu.SemaphoreType.DMA
    out = pl.pallas_call(
        functools.partial(general_kernel, groups, spaces),
        out_shape=jax.ShapeDtypeStruct((block, 2 * rows, total), jnp.float32),
        in_specs=[
            pl.BlockSpec(memory_space=pltpu.SMEM),
            pl.BlockSpec(memory_space=pltpu.SMEM),
            pl.BlockSpec(memory_space=pltpu.VMEM),
        ],
        out_specs=pl.BlockSpec(memory_space=pltpu.VMEM),
        scratch_shapes=[
            pltpu.VMEM((groups, 6, block, site_count), jnp.bfloat16),
            pltpu.VMEM((6, total, site_count), jnp.float32),
            pltpu.VMEM((6 * site_count, 2 * total), jnp.bfloat16),
            pltpu.VMEM((SLOTS * total, 6 * site_count), jnp.bfloat16),
            pltpu.VMEM((steps, 2, planes, SLOTS, 2 * rows, total), jnp.float32),
            pltpu.VMEM((steps, planes, SLOTS, 2 * rows, total), jnp.bfloat16),
            pltpu.VMEM((steps, planes, SLOTS, 2 * rows, total), jnp.bfloat16),
            pltpu.VMEM((steps, planes, SLOTS, 2 * rows, total), jnp.bfloat16),
            pltpu.VMEM((planes - 1, steps, SLOTS, 2 * rows, total), jnp.bfloat16),
            dma,
            dma((max(groups - 1, 6),)),
            dma((max(groups - 1, 6),)),
            dma((steps,)),
            dma((steps,)),
            dma((planes - 1, steps)),
            dma((planes - 1, steps)),
        ],
        compiler_params=pltpu.CompilerParams(
            collective_id=0, has_side_effects=True, vmem_limit_bytes=48 * 1024 * 1024
        ),
    )(assignment, momentum, mine)
    return jnp.transpose(out.reshape(block, 2, rows, total), (2, 1, 0, 3))


GROUPS = 4
SPACES = 8
PLANES = 4
BLOCK = 32
TOTAL = 128
SITES = 512
SPAN = 3 * SITES
QUADS = 4
CHUNK = 8
LAG = 4
TILES = SITES // LANES
SLICE = 3 * LANES
STEPS = TOTAL // 2 // CHUNK
CHUNK_ROWS = CHUNK * BLOCK
QUAD_ROWS = CHUNK * BLOCK // QUADS
WINDOW = BLOCK + TOTAL // 2
PART = WINDOW // QUADS
DISTANCES = TOTAL // 2


def ring(position):
    return position + lax.div(position, 2) * (1 - 2 * lax.rem(position, 2))


def fast_kernel(
    slots_any,
    momentum_any,
    block_any,
    out_ref,
    slots_ref,
    momentum_ref,
    block_ref,
    mine,
    gathered,
    wide,
    turned,
    turns,
    pick,
    in_order,
    placed,
    weighted,
    part,
    pair_out,
    part_in,
    sums,
    rounded,
    rounded_in,
    swap_out,
    swap_one,
    swap_two,
    extended,
    assembled,
    spots,
    local_sem,
    own_sem,
    known_sem,
    gather_send,
    gather_recv,
    pair_send,
    pair_recv,
    sum_send,
    sum_recv,
    swap_send,
    swap_recv,
):
    scale = jnp.float32(1.0 / math.sqrt(SITES * SPACES))
    group = lax.axis_index("group")
    space = lax.axis_index("space")
    core = lax.rem(space, 2)
    plane = lax.div(space, 2)
    position = ring(group)

    loads = [
        pltpu.make_async_copy(block_any, block_ref, local_sem.at[0]),
        pltpu.make_async_copy(slots_any, slots_ref, local_sem.at[1]),
        pltpu.make_async_copy(momentum_any, momentum_ref, local_sem.at[2]),
    ]
    for load in loads:
        load.start()

    barrier = pltpu.get_barrier_semaphore()
    beside = group + 1 - 2 * lax.rem(group, 2)
    across = group + 2 - 4 * lax.div(group, 2)
    partner = plane + 1 - 2 * lax.rem(plane, 2)
    mirror = PLANES - 1 - plane
    second = lax.rem(plane + 2, PLANES)
    middle = lax.div(plane + 1, 2) == 1

    def at_plane(target):
        return {"space": target * 2 + core}

    def greet(semaphore, device):
        pl.semaphore_signal(semaphore, inc=1, device_id=device, device_id_type=MESH)

    greet(barrier, {"space": plane * 2 + 1 - core})
    greet(barrier, {"group": beside})
    greet(barrier, {"group": across})
    greet(barrier, at_plane(partner))

    @pl.when(middle)
    def _():
        greet(barrier, at_plane(mirror))

    loads[0].wait()
    for tile in range(TILES):
        for k in range(4):
            for a in range(3):
                rows = block_ref[8 * k : 8 * k + 8, a, :, tile * LANES : (tile + 1) * LANES]
                first = (k % 2) * 16
                mine[tile, k // 2, first : first + 16, a * LANES : (a + 1) * LANES] = rows.reshape(
                    16, LANES
                )
    own = pltpu.make_async_copy(mine, gathered.at[:, :, group, :, :SLICE], own_sem)
    own.start()

    @pl.when(middle)
    def _():
        pl.semaphore_wait(barrier, 5)
        greet(known_sem, at_plane(mirror))

    @pl.when(jnp.logical_not(middle))
    def _():
        pl.semaphore_wait(barrier, 4)

    def gather_copy(tile, lane, target, source, half, owner):
        return pltpu.make_async_remote_copy(
            src_ref=source,
            dst_ref=gathered.at[tile, half, owner, :, :SLICE],
            send_sem=gather_send.at[tile, lane],
            recv_sem=gather_recv.at[tile, lane],
            device_id={"group": target},
            device_id_type=MESH,
        )

    def leading(tile):
        return [
            gather_copy(tile, 0, beside, mine.at[tile, 0], 0, group),
            gather_copy(tile, 1, across, mine.at[tile, 1], 1, group),
        ]

    def trailing(tile):
        return [
            gather_copy(tile, 2, beside, mine.at[tile, 1], 1, group),
            gather_copy(tile, 3, across, mine.at[tile, 0], 0, group),
        ]

    def onward(tile):
        return [
            gather_copy(tile, 4, across, gathered.at[tile, 0, beside, :, :SLICE], 0, beside),
            gather_copy(tile, 5, beside, gathered.at[tile, 1, across, :, :SLICE], 1, across),
        ]

    def pass_on(tile):
        for copy, further in zip(leading(tile), onward(tile)):
            copy.wait_recv()
            further.start()

    for tile in range(TILES - 1):
        for copy in leading(tile) + trailing(tile):
            copy.start()

    for load in loads[1:]:
        load.wait()
    sites = space * SITES + lax.broadcasted_iota(jnp.int32, (8, SITES), 1)
    coord_x = sites & (L - 1)
    coord_y = (sites >> 6) & (L - 1)
    coord_z = sites >> 12
    phase = momentum_ref[0] * coord_x + momentum_ref[1] * coord_y + momentum_ref[2] * coord_z
    angle = (phase & (L - 1)).astype(jnp.float32) * jnp.float32(2.0 * math.pi / L)
    cosine = jnp.cos(angle)
    sine = jnp.sin(angle)
    for tile in range(TILES):
        turns[0, tile] = cosine[:, tile * LANES : (tile + 1) * LANES]
        turns[1, tile] = sine[:, tile * LANES : (tile + 1) * LANES]

    in_order[...] = jnp.broadcast_to(slots_ref[...].astype(jnp.float32), (TOTAL, LANES)).T.astype(jnp.int32)
    for block in range(GROUPS):
        first = pl.multiple_of(ring(lax.rem(position + block, GROUPS)) * BLOCK, BLOCK)
        value = in_order[pl.ds(first, BLOCK), :]
        placed[block * BLOCK : (block + 1) * BLOCK, :] = value
        placed[TOTAL + block * BLOCK : TOTAL + (block + 1) * BLOCK, :] = value

    own.wait()
    pass_on(0)
    for copy in leading(TILES - 1) + trailing(TILES - 1):
        copy.start()
    lane = lax.broadcasted_iota(jnp.int32, (PART, 2 * TOTAL), 1)
    lane_vector = (2 * ((lane // BLOCK) % GROUPS) + lane // TOTAL) * 16 + (lane // 2) % 16
    picks = []
    for c in range(2):
        for q in range(QUADS):
            wanted = placed[pl.ds(q, PART, stride=QUADS), :]
            wanted = jnp.concatenate([wanted, wanted], axis=1)
            hit = jnp.logical_and(lane_vector == wanted, lane % 2 == c)
            picks.append(jnp.where(hit, 1.0, 0.0).astype(jnp.float32))
    row = lax.broadcasted_iota(jnp.int32, (2 * TOTAL, 2 * TOTAL), 0)
    column = lax.broadcasted_iota(jnp.int32, (2 * TOTAL, 2 * TOTAL), 1)
    other = row + 1 - 2 * (row % 2)
    sign = (2 * (row % 2) - 1).astype(jnp.float32)
    picks.append(jnp.where(column == other, sign, 0.0))
    pick[...] = jnp.concatenate(picks, axis=0).astype(jnp.bfloat16)

    pass_on(1)
    pass_on(2)

    def arrived(tile):
        for copy in trailing(tile) + onward(tile):
            copy.wait_recv()

    def prepare(tile):
        rows = gathered[tile, :, :, :, :SLICE].reshape(2 * TOTAL, SLICE)
        table = jnp.dot(pick[...], rows, preferred_element_type=jnp.float32)
        gathered[tile, :, :, :, SLICE:] = (
            table[2 * QUADS * PART :].astype(jnp.bfloat16).reshape(2, GROUPS, BLOCK, SLICE)
        )
        for q in range(QUADS):
            for a in range(3):
                first = q * PART
                at = slice(a * LANES, (a + 1) * LANES)
                re = table[first : first + PART, at]
                im = table[QUADS * PART + first : QUADS * PART + first + PART, at]
                wide[a, tile, q] = re
                wide[3 + a, tile, q] = im
                wide[6 + a, tile, q] = re + im
                re, im = re[:8], im[:8]
                turn_re = re * turns[0, tile] - im * turns[1, tile]
                turn_im = re * turns[1, tile] + im * turns[0, tile]
                turned[a, tile, q] = turn_re
                turned[3 + a, tile, q] = turn_im
                turned[6 + a, tile, q] = turn_re + turn_im

    def fill(step, tile, count, into):
        for q in range(QUADS):
            turn = [turned[c, tile, q] for c in range(9)]
            for pair in range(count // 2):
                crosses = []
                for k in range(2):
                    on = q + 1 + 2 * pair + k
                    at = pl.ds((count // QUADS) * step + on // QUADS, 8)
                    side = [wide[c, tile, on % QUADS, at] for c in range(9)]
                    made = []
                    for a in range(3):
                        b, c = (a + 1) % 3, (a + 2) % 3
                        re, im, both = (
                            side[n + b] * turn[n + c] - side[n + c] * turn[n + b] for n in (0, 3, 6)
                        )
                        made += [re - im, both - (re + im)]
                    crosses.append(made)
                top = (q * count // 2 + pair) * 16
                for a in range(3):
                    for c in range(2):
                        both = jnp.concatenate([crosses[k][2 * a + c] for k in range(2)], axis=0)
                        base = (c * 3 + a) * LANES
                        into[top : top + 16, base : base + LANES] = both.astype(jnp.bfloat16)

    def times(values, tile):
        return lax.dot_general(
            values,
            gathered[tile].reshape(2 * TOTAL, 2 * SLICE),
            (((1,), (1,)), ((), ())),
            preferred_element_type=jnp.float32,
        )

    def early(step, carry):
        fill(STEPS - 1 - step, 0, CHUNK, weighted.at[0])
        value = times(weighted[0], 0)
        for h in range(2):
            part[step, h] = value[:, h * LANES : (h + 1) * LANES]

        @pl.when(step == 0)
        def _():
            pass_on(TILES - 1)

        return carry

    arrived(0)
    prepare(0)
    lax.fori_loop(0, STEPS, early, 0)
    for tile in range(1, TILES):
        arrived(tile)
        prepare(tile)
    for tile in range(TILES):
        for copy in leading(tile) + trailing(tile) + onward(tile):
            copy.wait_send()

    @pl.when(middle)
    def _():
        pl.semaphore_wait(known_sem, 1)
        greet(known_sem, at_plane(partner))

    @pl.when(jnp.logical_not(middle))
    def _():
        pl.semaphore_wait(known_sem, 1)

    def pair_copy(step):
        return pltpu.make_async_remote_copy(
            src_ref=pair_out.at[step],
            dst_ref=part_in.at[step],
            send_sem=pair_send.at[step],
            recv_sem=pair_recv.at[step],
            device_id={"space": plane * 2 + 1 - core},
            device_id_type=MESH,
        )

    def sum_copy(step, lane, source, slot, target):
        return pltpu.make_async_remote_copy(
            src_ref=source,
            dst_ref=rounded_in.at[slot, step],
            send_sem=sum_send.at[lane, step],
            recv_sem=sum_recv.at[slot, step],
            device_id=at_plane(target),
            device_id_type=MESH,
        )

    def onto(step):
        return [
            sum_copy(step, n, rounded.at[step, target], n, target)
            for n, target in enumerate((mirror, second, partner))
        ]

    def swap_copy(chunk, rows, reach):
        rows = pl.ds(rows.start, rows.stop - rows.start)
        return pltpu.make_async_remote_copy(
            src_ref=swap_out.at[chunk, rows],
            dst_ref=(swap_one if reach == 1 else swap_two).at[chunk, rows],
            send_sem=swap_send.at[reach - 1, chunk],
            recv_sem=swap_recv.at[reach - 1, chunk],
            device_id={"group": ring(lax.rem(position + reach, GROUPS))},
            device_id_type=MESH,
        )

    def quad_of(shape):
        return lax.broadcasted_iota(jnp.int32, shape, len(shape) - 1) // 32

    def forward(step):
        pair_copy(step).wait()
        quad = quad_of((QUAD_ROWS, LANES))
        held = []
        for q in range(QUADS):
            at = slice(q * QUAD_ROWS, (q + 1) * QUAD_ROWS)
            held.append(part[step, core, at] + part_in[step, at].astype(jnp.float32))
        for shift in (64, 32):
            low = (quad * 32 // shift) % 2 == 0
            apart = shift // 32
            for q in range(QUADS):
                if (q // apart) % 2 == 0:
                    one, two = held[q], held[q + apart]
                    held[q] = jnp.where(low, one, pltpu.roll(two, shift, 1))
                    held[q + apart] = jnp.where(low, pltpu.roll(one, LANES - shift, 1), two)
        for t in range(PLANES):
            sums[step, t] = held[t]
            rounded[step, t] = held[t].astype(jnp.bfloat16)
        for copy in onto(step):
            copy.start()

    half_rows = QUAD_ROWS // 2
    low_rows, high_rows = slice(0, half_rows), slice(half_rows, QUAD_ROWS)
    all_rows = slice(0, QUAD_ROWS)

    def reaches(chunk):
        one = high_rows if chunk < 2 else all_rows if chunk < 6 else low_rows
        two = None if chunk < 4 else high_rows if chunk < 6 else all_rows
        return one, two

    def finish(step):
        chunk = STEPS - 1 - step
        value = sums[step, plane]
        for n, copy in enumerate(onto(step)):
            copy.wait_recv()
            value = value + rounded_in[n, step].astype(jnp.float32)
        first = 16 * DISTANCES + chunk * CHUNK
        for k in range(CHUNK):
            extended[pl.ds(first + k, 8, stride=DISTANCES), :] = value[8 * k : 8 * k + 8]
        for k in range(0, 8, 2):
            both = [
                extended[pl.ds(pl.multiple_of(first + n * DISTANCES, CHUNK), CHUNK), :]
                for n in (k, k + 1)
            ]
            swap_out[chunk, 8 * k : 8 * k + 16] = jnp.concatenate(both, axis=0).astype(jnp.bfloat16)

        for low, high in ((0, 2), (2, 4), (4, 6), (6, 8)):

            @pl.when(jnp.logical_and(chunk >= low, chunk < high))
            def _():
                one, two = reaches(low)
                swap_copy(chunk, one, 1).start()
                if two is not None:
                    swap_copy(chunk, two, 2).start()

    def body(step, carry):
        def one(n, inner):
            fill(STEPS - 1 - step, 1 + n, CHUNK, weighted.at[n])
            return inner

        lax.fori_loop(0, TILES - 1, one, 0)
        value = times(weighted[0], 1)
        for n in range(1, TILES - 1):
            value = value + times(weighted[n], 1 + n)
        for h in range(2):
            part[step, h] += value[:, h * LANES : (h + 1) * LANES]
        pair_out[step] = part[step, 1 - core].astype(jnp.bfloat16)
        pair_copy(step).start()

        @pl.when(step >= 1)
        def _():
            forward(step - 1)

        @pl.when(step >= LAG)
        def _():
            finish(step - LAG)

        return carry

    lax.fori_loop(0, STEPS, body, 0)
    forward(STEPS - 1)

    columns = lax.broadcasted_iota(jnp.int32, (TOTAL, TOTAL), 1)
    for row in range(8):
        spot = jnp.where(placed[QUADS * row : QUADS * row + TOTAL, :] == columns, 1.0, 0.0)
        spots[row, :TOTAL] = spot.astype(jnp.bfloat16)
        spots[row, TOTAL:] = spot.astype(jnp.bfloat16)

    def last(step, carry):
        finish(step)
        return carry

    lax.fori_loop(STEPS - LAG, STEPS, last, 0)
    for step in range(STEPS):
        for copy in onto(step):
            copy.wait_send()

    quad = quad_of((8, LANES))

    def at_distance(d):
        if d > 0:
            return extended[pl.ds(16 * DISTANCES + d - 1, 8, stride=DISTANCES), :]
        if d == 0:
            return jnp.zeros((8, LANES), jnp.float32)
        row, rest = divmod(TOTAL // 2 + d, QUADS)
        value = extended[pl.ds(row * DISTANCES - d - 1, 8, stride=DISTANCES), :]
        if rest:
            later = extended[pl.ds((row + 1) * DISTANCES - d - 1, 8, stride=DISTANCES), :]
            value = pltpu.roll(jnp.where(quad >= rest, value, later), LANES - 32 * rest, 1)
        return -value

    def wrapped(d):
        return d - TOTAL if d > TOTAL // 2 else d

    def land(chunk):
        for reach, rows in enumerate(reaches(chunk), 1):
            if rows is None:
                continue
            swap_copy(chunk, rows, reach).wait()
            came = (swap_one if reach == 1 else swap_two)[chunk, rows].astype(jnp.float32)
            for n in range((rows.stop - rows.start) // 8):
                row = (2 - reach) * 8 + rows.start // 8 + n
                first = row * DISTANCES + chunk * CHUNK
                extended[first : first + CHUNK, :] = came[8 * n : 8 * n + 8]

    def place(first, stop):
        recent = [at_distance(wrapped(d)) for d in range(first - QUADS + 1, first)]
        for e in range(first, stop):
            recent.append(at_distance(wrapped(e)))
            value = recent[-1]
            for q in range(1, QUADS):
                value = jnp.where(quad == q, recent[-1 - q], value)
            row = e % TOTAL
            assembled[row * 8 : row * 8 + 8, :] = value

    for chunk in reversed(range(1, STEPS)):
        land(chunk)
    place(QUADS - TOTAL // 2, -CHUNK)
    place(QUADS, TOTAL // 2 + QUADS)
    land(0)
    place(-CHUNK, QUADS)

    for row in range(8):
        piece = assembled[pl.ds(row, TOTAL, stride=8), :].T
        high = piece.astype(jnp.bfloat16)
        low = (piece - high.astype(jnp.float32)).astype(jnp.bfloat16)
        moved = jnp.dot(
            jnp.concatenate([high, low], axis=1),
            spots[row],
            preferred_element_type=jnp.float32,
        )
        moved = moved * scale
        for q in range(QUADS):
            out_ref[pl.ds(QUADS * row + q, 32, stride=BLOCK), :] = moved[32 * q : 32 * q + 32]


def fast(vectors, momentum, assignment):
    mine = jnp.transpose(vectors, (0, 2, 1, 3))
    dma = pltpu.SemaphoreType.DMA
    f32, b16 = jnp.float32, jnp.bfloat16
    out = pl.pallas_call(
        fast_kernel,
        out_shape=jax.ShapeDtypeStruct((32 * BLOCK, TOTAL), f32),
        in_specs=[
            pl.BlockSpec(memory_space=pl.ANY),
            pl.BlockSpec(memory_space=pl.ANY),
            pl.BlockSpec(memory_space=pl.ANY),
        ],
        out_specs=pl.BlockSpec(memory_space=pltpu.VMEM),
        scratch_shapes=[
            pltpu.VMEM((1, TOTAL), jnp.int32),
            pltpu.SMEM((3,), jnp.int32),
            pltpu.VMEM((BLOCK, 3, 2, SITES), b16),
            pltpu.VMEM((TILES, 2, BLOCK, SLICE), b16),
            pltpu.VMEM((TILES, 2, GROUPS, BLOCK, 2 * SLICE), b16),
            pltpu.VMEM((9, TILES, QUADS, PART, LANES), f32),
            pltpu.VMEM((9, TILES, QUADS, 8, LANES), f32),
            pltpu.VMEM((2, TILES, 8, LANES), f32),
            pltpu.VMEM((2 * QUADS * PART + 2 * TOTAL, 2 * TOTAL), b16),
            pltpu.VMEM((TOTAL, LANES), jnp.int32),
            pltpu.VMEM((2 * TOTAL, LANES), jnp.int32),
            pltpu.VMEM((TILES - 1, CHUNK_ROWS, 2 * SLICE), b16),
            pltpu.VMEM((STEPS, 2, CHUNK_ROWS, LANES), f32),
            pltpu.VMEM((STEPS, CHUNK_ROWS, LANES), b16),
            pltpu.VMEM((STEPS, CHUNK_ROWS, LANES), b16),
            pltpu.VMEM((STEPS, PLANES, QUAD_ROWS, LANES), f32),
            pltpu.VMEM((STEPS, PLANES, QUAD_ROWS, LANES), b16),
            pltpu.VMEM((PLANES - 1, STEPS, QUAD_ROWS, LANES), b16),
            pltpu.VMEM((STEPS, QUAD_ROWS, LANES), b16),
            pltpu.VMEM((STEPS, QUAD_ROWS, LANES), b16),
            pltpu.VMEM((STEPS, QUAD_ROWS, LANES), b16),
            pltpu.VMEM((24 * DISTANCES, LANES), f32),
            pltpu.VMEM((8 * TOTAL, LANES), f32),
            pltpu.VMEM((8, 2 * TOTAL, TOTAL), b16),
            dma((3,)),
            dma,
            pltpu.SemaphoreType.REGULAR,
            dma((TILES, 6)),
            dma((TILES, 6)),
            dma((STEPS,)),
            dma((STEPS,)),
            dma((PLANES - 1, STEPS)),
            dma((PLANES - 1, STEPS)),
            dma((2, STEPS)),
            dma((2, STEPS)),
        ],
        compiler_params=pltpu.CompilerParams(
            collective_id=0, has_side_effects=True, vmem_limit_bytes=48 * 1024 * 1024
        ),
    )(assignment.reshape(1, TOTAL), momentum, mine)
    return out.reshape(16, 2, BLOCK, TOTAL)


def local(groups, spaces, vectors, momentum, assignment):
    if (groups, spaces) == (GROUPS, SPACES) and vectors.shape == (BLOCK, 2, 3, SITES):
        return fast(vectors, momentum, assignment)
    return general(groups, spaces, vectors, momentum, assignment)


def solution(mesh):
    return jax.shard_map(
        functools.partial(local, mesh.shape["group"], mesh.shape["space"]),
        mesh=mesh,
        in_specs=(P("group", None, None, "space"), P(), P()),
        out_specs=P("space", None, "group", None),
        check_vma=False,
    )
```

```python
import functools
import math

import jax
import jax.numpy as jnp
from jax import lax
from jax.experimental import pallas as pl
from jax.experimental.pallas import tpu as pltpu
from jax.sharding import PartitionSpec as P

L = 64
MESH = pl.DeviceIdType.MESH
LANES = 128
ROWS = 16
SLOTS = 4


def general_kernel(
    groups,
    spaces,
    slots_ref,
    momentum_ref,
    block_ref,
    out_ref,
    gathered,
    wide,
    right,
    weighted,
    part,
    pair_out,
    part_in,
    rounded,
    rounded_in,
    local_sem,
    gather_send,
    gather_recv,
    pair_send,
    pair_recv,
    sum_send,
    sum_recv,
):
    block = block_ref.shape[1]
    site_count = block_ref.shape[2]
    total = groups * block
    rows = total // spaces
    planes = spaces // 2
    steps = block // SLOTS
    span = 3 * site_count
    scale = jnp.float32(1.0 / math.sqrt(site_count * spaces))
    group = lax.axis_index("group")
    space = lax.axis_index("space")
    core = lax.rem(space, 2)
    plane = lax.div(space, 2)

    barrier = pltpu.get_barrier_semaphore()
    for off in range(1, groups):
        pl.semaphore_signal(
            barrier, inc=1, device_id={"group": lax.rem(group + off, groups)}, device_id_type=MESH
        )
    for off in range(1, planes):
        pl.semaphore_signal(
            barrier,
            inc=1,
            device_id={"space": lax.rem(plane + off, planes) * 2 + core},
            device_id_type=MESH,
        )
    pl.semaphore_signal(
        barrier, inc=1, device_id={"space": plane * 2 + 1 - core}, device_id_type=MESH
    )
    pl.semaphore_wait(barrier, groups + planes - 1)

    def gather_copy(lane, target, source, owner, first, count):
        at = pl.ds(first, count)
        return pltpu.make_async_remote_copy(
            src_ref=source.at[at],
            dst_ref=gathered.at[owner, at],
            send_sem=gather_send.at[lane],
            recv_sem=gather_recv.at[lane],
            device_id={"group": target},
            device_id_type=MESH,
        )

    square = groups == 4
    if square:
        beside = group + 1 - 2 * lax.rem(group, 2)
        across = group + 2 - 4 * lax.div(group, 2)
        sends = [
            gather_copy(0, beside, block_ref, group, 0, 3),
            gather_copy(1, across, block_ref, group, 3, 3),
            gather_copy(2, beside, block_ref, group, 3, 3),
            gather_copy(3, across, block_ref, group, 0, 3),
        ]
        passed = [
            gather_copy(4, across, gathered.at[beside], beside, 0, 3),
            gather_copy(5, beside, gathered.at[across], across, 3, 3),
        ]
    else:
        sends = [
            gather_copy(off - 1, lax.rem(group + off, groups), block_ref, group, 0, 6)
            for off in range(1, groups)
        ]
    for copy in sends:
        copy.start()
    own = pltpu.make_async_copy(block_ref, gathered.at[group], local_sem)
    own.start()
    if square:
        for copy, onward in zip(sends, passed):
            copy.wait_recv()
            onward.start()

    sites = space * site_count + lax.broadcasted_iota(jnp.int32, (8, site_count), 1)
    coord_x = sites & (L - 1)
    coord_y = (sites >> 6) & (L - 1)
    coord_z = sites >> 12
    phase = momentum_ref[0] * coord_x + momentum_ref[1] * coord_y + momentum_ref[2] * coord_z
    angle = (phase & (L - 1)).astype(jnp.float32) * jnp.float32(2.0 * math.pi / L)
    cosine = jnp.cos(angle)[0:1]
    sine = jnp.sin(angle)[0:1]

    own.wait()
    if square:
        for copy in sends[:2]:
            copy.wait_send()
        for copy in sends[2:] + passed:
            copy.wait()
    else:
        for copy in sends:
            copy.wait()

    for q in range(groups):
        for c in range(6):
            wide[c, q * block : (q + 1) * block, :] = gathered[q, c].astype(jnp.float32)

    for a in range(3):
        real = wide[a].T.astype(jnp.bfloat16)
        imag = wide[3 + a].T.astype(jnp.bfloat16)
        low, high = a * site_count, (a + 1) * site_count
        right[low:high, :total] = real
        right[low:high, total:] = imag
        right[span + low : span + high, :total] = -imag
        right[span + low : span + high, total:] = real

    def fill(step, first, stop):
        def one(half, carry):
            k = slots_ref[group * block + SLOTS * step + half]
            row = [wide[c, pl.ds(k, 1), :] for c in range(6)]
            turn_re = [row[a] * cosine - row[3 + a] * sine for a in range(3)]
            turn_im = [row[a] * sine + row[3 + a] * cosine for a in range(3)]

            def tile(j, inner):
                top = pl.multiple_of(j * ROWS, ROWS)
                for s in range(0, site_count, LANES):
                    cols = slice(s, s + LANES)
                    re = [wide[a, pl.ds(top, ROWS), cols] for a in range(3)]
                    im = [wide[3 + a, pl.ds(top, ROWS), cols] for a in range(3)]
                    tr = [x[:, cols] for x in turn_re]
                    ti = [x[:, cols] for x in turn_im]
                    for a in range(3):
                        b, c = (a + 1) % 3, (a + 2) % 3
                        out_re = (re[b] * tr[c] - im[b] * ti[c]) - (re[c] * tr[b] - im[c] * ti[b])
                        out_im = (re[b] * ti[c] + im[b] * tr[c]) - (re[c] * ti[b] + im[c] * tr[b])
                        base = a * site_count + s
                        at = pl.ds(pl.multiple_of(half * total + top, ROWS), ROWS)
                        weighted[at, base : base + LANES] = out_re.astype(jnp.bfloat16)
                        weighted[at, span + base : span + base + LANES] = out_im.astype(jnp.bfloat16)
                return inner

            return lax.fori_loop(0, total // ROWS, tile, carry, unroll=True)

        lax.fori_loop(first, stop, one, 0)

    def pair_copy(step):
        return pltpu.make_async_remote_copy(
            src_ref=pair_out.at[step],
            dst_ref=part_in.at[step],
            send_sem=pair_send.at[step],
            recv_sem=pair_recv.at[step],
            device_id={"space": plane * 2 + 1 - core},
            device_id_type=MESH,
        )

    def sum_copy(step, off):
        target = lax.rem(plane + off, planes)
        return pltpu.make_async_remote_copy(
            src_ref=rounded.at[step, target],
            dst_ref=rounded_in.at[off - 1, step],
            send_sem=sum_send.at[off - 1, step],
            recv_sem=sum_recv.at[off - 1, step],
            device_id={"space": target * 2 + core},
            device_id_type=MESH,
        )

    def forward(step):
        pair_copy(step).wait()
        rounded[step] = (part[step, core] + part_in[step].astype(jnp.float32)).astype(jnp.bfloat16)
        for off in range(1, planes):
            sum_copy(step, off).start()
        out_ref[pl.ds(SLOTS * step, SLOTS)] = part[step, core, plane] + part_in[step, plane].astype(jnp.float32)

    def body(step, carry):
        fill(step, 0, SLOTS - 1)

        @pl.when(step >= 1)
        def _():
            forward(step - 1)

        fill(step, SLOTS - 1, SLOTS)
        product = jnp.dot(weighted[...], right[...], preferred_element_type=jnp.float32)
        for half in range(SLOTS):
            piece = product[half * total : (half + 1) * total].T
            for c in range(2):
                for i in range(spaces):
                    first = c * total + i * rows
                    part[step, i % 2, i // 2, half, c * rows : (c + 1) * rows] = piece[
                        first : first + rows
                    ]
        pair_out[step] = part[step, 1 - core].astype(jnp.bfloat16)
        pair_copy(step).start()

        return carry

    lax.fori_loop(0, steps, body, 0)
    forward(steps - 1)

    def finish(step, carry):
        value = out_ref[pl.ds(SLOTS * step, SLOTS)]
        for off in range(1, planes):
            sum_copy(step, off).wait()
            value = value + rounded_in[off - 1, step].astype(jnp.float32)
        out_ref[pl.ds(SLOTS * step, SLOTS)] = value * scale
        return carry

    lax.fori_loop(0, steps, finish, 0)


def general(groups, spaces, vectors, momentum, assignment):
    block, _, _, site_count = vectors.shape
    total = block * groups
    rows = total // spaces
    planes = spaces // 2
    steps = block // SLOTS
    mine = jnp.transpose(vectors, (1, 2, 0, 3)).reshape(6, block, site_count)
    dma = pltpu.SemaphoreType.DMA
    out = pl.pallas_call(
        functools.partial(general_kernel, groups, spaces),
        out_shape=jax.ShapeDtypeStruct((block, 2 * rows, total), jnp.float32),
        in_specs=[
            pl.BlockSpec(memory_space=pltpu.SMEM),
            pl.BlockSpec(memory_space=pltpu.SMEM),
            pl.BlockSpec(memory_space=pltpu.VMEM),
        ],
        out_specs=pl.BlockSpec(memory_space=pltpu.VMEM),
        scratch_shapes=[
            pltpu.VMEM((groups, 6, block, site_count), jnp.bfloat16),
            pltpu.VMEM((6, total, site_count), jnp.float32),
            pltpu.VMEM((6 * site_count, 2 * total), jnp.bfloat16),
            pltpu.VMEM((SLOTS * total, 6 * site_count), jnp.bfloat16),
            pltpu.VMEM((steps, 2, planes, SLOTS, 2 * rows, total), jnp.float32),
            pltpu.VMEM((steps, planes, SLOTS, 2 * rows, total), jnp.bfloat16),
            pltpu.VMEM((steps, planes, SLOTS, 2 * rows, total), jnp.bfloat16),
            pltpu.VMEM((steps, planes, SLOTS, 2 * rows, total), jnp.bfloat16),
            pltpu.VMEM((planes - 1, steps, SLOTS, 2 * rows, total), jnp.bfloat16),
            dma,
            dma((max(groups - 1, 6),)),
            dma((max(groups - 1, 6),)),
            dma((steps,)),
            dma((steps,)),
            dma((planes - 1, steps)),
            dma((planes - 1, steps)),
        ],
        compiler_params=pltpu.CompilerParams(
            collective_id=0, has_side_effects=True, vmem_limit_bytes=48 * 1024 * 1024
        ),
    )(assignment, momentum, mine)
    return jnp.transpose(out.reshape(block, 2, rows, total), (2, 1, 0, 3))


GROUPS = 4
SPACES = 8
PLANES = 4
BLOCK = 32
TOTAL = 128
SITES = 512
SPAN = 3 * SITES
QUADS = 4
CHUNK = 8
LAG = 4
TILES = SITES // LANES
SLICE = 3 * LANES
STEPS = TOTAL // 2 // CHUNK
CHUNK_ROWS = CHUNK * BLOCK
QUAD_ROWS = CHUNK * BLOCK // QUADS
WINDOW = BLOCK + TOTAL // 2
PART = WINDOW // QUADS
DISTANCES = TOTAL // 2


def ring(position):
    return position + lax.div(position, 2) * (1 - 2 * lax.rem(position, 2))


def fast_kernel(
    slots_any,
    momentum_any,
    block_any,
    out_ref,
    slots_ref,
    momentum_ref,
    block_ref,
    mine,
    gathered,
    wide,
    turned,
    turns,
    pick,
    in_order,
    placed,
    weighted,
    part,
    pair_out,
    part_in,
    sums,
    rounded,
    rounded_in,
    swap_out,
    swap_one,
    swap_two,
    extended,
    assembled,
    spots,
    local_sem,
    own_sem,
    known_sem,
    gather_send,
    gather_recv,
    pair_send,
    pair_recv,
    sum_send,
    sum_recv,
    swap_send,
    swap_recv,
):
    scale = jnp.float32(1.0 / math.sqrt(SITES * SPACES))
    group = lax.axis_index("group")
    space = lax.axis_index("space")
    core = lax.rem(space, 2)
    plane = lax.div(space, 2)
    position = ring(group)

    loads = [
        pltpu.make_async_copy(block_any, block_ref, local_sem.at[0]),
        pltpu.make_async_copy(slots_any, slots_ref, local_sem.at[1]),
        pltpu.make_async_copy(momentum_any, momentum_ref, local_sem.at[2]),
    ]
    for load in loads:
        load.start()

    barrier = pltpu.get_barrier_semaphore()
    beside = group + 1 - 2 * lax.rem(group, 2)
    across = group + 2 - 4 * lax.div(group, 2)
    partner = plane + 1 - 2 * lax.rem(plane, 2)
    mirror = PLANES - 1 - plane
    second = lax.rem(plane + 2, PLANES)
    middle = lax.div(plane + 1, 2) == 1

    def at_plane(target):
        return {"space": target * 2 + core}

    def greet(semaphore, device):
        pl.semaphore_signal(semaphore, inc=1, device_id=device, device_id_type=MESH)

    greet(barrier, {"space": plane * 2 + 1 - core})
    greet(barrier, {"group": beside})
    greet(barrier, {"group": across})
    greet(barrier, at_plane(partner))

    @pl.when(middle)
    def _():
        greet(barrier, at_plane(mirror))

    loads[0].wait()
    for tile in range(TILES):
        for k in range(4):
            for a in range(3):
                rows = block_ref[8 * k : 8 * k + 8, a, :, tile * LANES : (tile + 1) * LANES]
                first = (k % 2) * 16
                mine[tile, k // 2, first : first + 16, a * LANES : (a + 1) * LANES] = rows.reshape(
                    16, LANES
                )
    own = pltpu.make_async_copy(mine, gathered.at[:, :, group, :, :SLICE], own_sem)
    own.start()

    @pl.when(middle)
    def _():
        pl.semaphore_wait(barrier, 5)
        greet(known_sem, at_plane(mirror))

    @pl.when(jnp.logical_not(middle))
    def _():
        pl.semaphore_wait(barrier, 4)

    def gather_copy(tile, lane, target, source, half, owner):
        return pltpu.make_async_remote_copy(
            src_ref=source,
            dst_ref=gathered.at[tile, half, owner, :, :SLICE],
            send_sem=gather_send.at[tile, lane],
            recv_sem=gather_recv.at[tile, lane],
            device_id={"group": target},
            device_id_type=MESH,
        )

    def leading(tile):
        return [
            gather_copy(tile, 0, beside, mine.at[tile, 0], 0, group),
            gather_copy(tile, 1, across, mine.at[tile, 1], 1, group),
        ]

    def trailing(tile):
        return [
            gather_copy(tile, 2, beside, mine.at[tile, 1], 1, group),
            gather_copy(tile, 3, across, mine.at[tile, 0], 0, group),
        ]

    def onward(tile):
        return [
            gather_copy(tile, 4, across, gathered.at[tile, 0, beside, :, :SLICE], 0, beside),
            gather_copy(tile, 5, beside, gathered.at[tile, 1, across, :, :SLICE], 1, across),
        ]

    def pass_on(tile):
        for copy, further in zip(leading(tile), onward(tile)):
            copy.wait_recv()
            further.start()

    for tile in range(TILES - 1):
        for copy in leading(tile) + trailing(tile):
            copy.start()

    for load in loads[1:]:
        load.wait()
    sites = space * SITES + lax.broadcasted_iota(jnp.int32, (8, SITES), 1)
    coord_x = sites & (L - 1)
    coord_y = (sites >> 6) & (L - 1)
    coord_z = sites >> 12
    phase = momentum_ref[0] * coord_x + momentum_ref[1] * coord_y + momentum_ref[2] * coord_z
    angle = (phase & (L - 1)).astype(jnp.float32) * jnp.float32(2.0 * math.pi / L)
    cosine = jnp.cos(angle)
    sine = jnp.sin(angle)
    for tile in range(TILES):
        turns[0, tile] = cosine[:, tile * LANES : (tile + 1) * LANES]
        turns[1, tile] = sine[:, tile * LANES : (tile + 1) * LANES]

    in_order[...] = jnp.broadcast_to(slots_ref[...].astype(jnp.float32), (TOTAL, LANES)).T.astype(jnp.int32)
    for block in range(GROUPS):
        first = pl.multiple_of(ring(lax.rem(position + block, GROUPS)) * BLOCK, BLOCK)
        value = in_order[pl.ds(first, BLOCK), :]
        placed[block * BLOCK : (block + 1) * BLOCK, :] = value
        placed[TOTAL + block * BLOCK : TOTAL + (block + 1) * BLOCK, :] = value

    own.wait()
    pass_on(0)
    for copy in leading(TILES - 1) + trailing(TILES - 1):
        copy.start()
    lane = lax.broadcasted_iota(jnp.int32, (PART, 2 * TOTAL), 1)
    lane_vector = (2 * ((lane // BLOCK) % GROUPS) + lane // TOTAL) * 16 + (lane // 2) % 16
    picks = []
    for c in range(2):
        for q in range(QUADS):
            wanted = placed[pl.ds(q, PART, stride=QUADS), :]
            wanted = jnp.concatenate([wanted, wanted], axis=1)
            hit = jnp.logical_and(lane_vector == wanted, lane % 2 == c)
            picks.append(jnp.where(hit, 1.0, 0.0).astype(jnp.float32))
    row = lax.broadcasted_iota(jnp.int32, (2 * TOTAL, 2 * TOTAL), 0)
    column = lax.broadcasted_iota(jnp.int32, (2 * TOTAL, 2 * TOTAL), 1)
    other = row + 1 - 2 * (row % 2)
    sign = (2 * (row % 2) - 1).astype(jnp.float32)
    picks.append(jnp.where(column == other, sign, 0.0))
    pick[...] = jnp.concatenate(picks, axis=0).astype(jnp.bfloat16)

    pass_on(1)
    pass_on(2)

    def arrived(tile):
        for copy in trailing(tile) + onward(tile):
            copy.wait_recv()

    def prepare(tile):
        rows = gathered[tile, :, :, :, :SLICE].reshape(2 * TOTAL, SLICE)
        table = jnp.dot(pick[...], rows, preferred_element_type=jnp.float32)
        gathered[tile, :, :, :, SLICE:] = (
            table[2 * QUADS * PART :].astype(jnp.bfloat16).reshape(2, GROUPS, BLOCK, SLICE)
        )
        for q in range(QUADS):
            for a in range(3):
                first = q * PART
                at = slice(a * LANES, (a + 1) * LANES)
                re = table[first : first + PART, at]
                im = table[QUADS * PART + first : QUADS * PART + first + PART, at]
                wide[a, tile, q] = re
                wide[3 + a, tile, q] = im
                wide[6 + a, tile, q] = re + im
                re, im = re[:8], im[:8]
                turn_re = re * turns[0, tile] - im * turns[1, tile]
                turn_im = re * turns[1, tile] + im * turns[0, tile]
                turned[a, tile, q] = turn_re
                turned[3 + a, tile, q] = turn_im
                turned[6 + a, tile, q] = turn_re + turn_im

    def fill(step, tile, count, into):
        for q in range(QUADS):
            turn = [turned[c, tile, q] for c in range(9)]
            for pair in range(count // 2):
                crosses = []
                for k in range(2):
                    on = q + 1 + 2 * pair + k
                    at = pl.ds((count // QUADS) * step + on // QUADS, 8)
                    side = [wide[c, tile, on % QUADS, at] for c in range(9)]
                    made = []
                    for a in range(3):
                        b, c = (a + 1) % 3, (a + 2) % 3
                        re, im, both = (
                            side[n + b] * turn[n + c] - side[n + c] * turn[n + b] for n in (0, 3, 6)
                        )
                        made += [re - im, both - (re + im)]
                    crosses.append(made)
                top = (q * count // 2 + pair) * 16
                for a in range(3):
                    for c in range(2):
                        both = jnp.concatenate([crosses[k][2 * a + c] for k in range(2)], axis=0)
                        base = (c * 3 + a) * LANES
                        into[top : top + 16, base : base + LANES] = both.astype(jnp.bfloat16)

    def times(values, tile):
        return lax.dot_general(
            values,
            gathered[tile].reshape(2 * TOTAL, 2 * SLICE),
            (((1,), (1,)), ((), ())),
            preferred_element_type=jnp.float32,
        )

    def early(step, carry):
        fill(STEPS - 1 - step, 0, CHUNK, weighted.at[0])
        value = times(weighted[0], 0)
        for h in range(2):
            part[step, h] = value[:, h * LANES : (h + 1) * LANES]

        @pl.when(step == 0)
        def _():
            pass_on(TILES - 1)

        return carry

    arrived(0)
    prepare(0)
    lax.fori_loop(0, STEPS, early, 0)
    for tile in range(1, TILES):
        arrived(tile)
        prepare(tile)
    for tile in range(TILES):
        for copy in leading(tile) + trailing(tile) + onward(tile):
            copy.wait_send()

    @pl.when(middle)
    def _():
        pl.semaphore_wait(known_sem, 1)
        greet(known_sem, at_plane(partner))

    @pl.when(jnp.logical_not(middle))
    def _():
        pl.semaphore_wait(known_sem, 1)

    def pair_copy(step):
        return pltpu.make_async_remote_copy(
            src_ref=pair_out.at[step],
            dst_ref=part_in.at[step],
            send_sem=pair_send.at[step],
            recv_sem=pair_recv.at[step],
            device_id={"space": plane * 2 + 1 - core},
            device_id_type=MESH,
        )

    def sum_copy(step, lane, source, slot, target):
        return pltpu.make_async_remote_copy(
            src_ref=source,
            dst_ref=rounded_in.at[slot, step],
            send_sem=sum_send.at[lane, step],
            recv_sem=sum_recv.at[slot, step],
            device_id=at_plane(target),
            device_id_type=MESH,
        )

    def onto(step):
        return [
            sum_copy(step, n, rounded.at[step, target], n, target)
            for n, target in enumerate((second, mirror, partner))
        ]

    def swap_copy(chunk, rows, reach):
        rows = pl.ds(rows.start, rows.stop - rows.start)
        return pltpu.make_async_remote_copy(
            src_ref=swap_out.at[chunk, rows],
            dst_ref=(swap_one if reach == 1 else swap_two).at[chunk, rows],
            send_sem=swap_send.at[reach - 1, chunk],
            recv_sem=swap_recv.at[reach - 1, chunk],
            device_id={"group": ring(lax.rem(position + reach, GROUPS))},
            device_id_type=MESH,
        )

    def quad_of(shape):
        return lax.broadcasted_iota(jnp.int32, shape, len(shape) - 1) // 32

    def forward(step):
        pair_copy(step).wait()
        quad = quad_of((QUAD_ROWS, LANES))
        held = []
        for q in range(QUADS):
            at = slice(q * QUAD_ROWS, (q + 1) * QUAD_ROWS)
            held.append(part[step, core, at] + part_in[step, at].astype(jnp.float32))
        for shift in (64, 32):
            low = (quad * 32 // shift) % 2 == 0
            apart = shift // 32
            for q in range(QUADS):
                if (q // apart) % 2 == 0:
                    one, two = held[q], held[q + apart]
                    held[q] = jnp.where(low, one, pltpu.roll(two, shift, 1))
                    held[q + apart] = jnp.where(low, pltpu.roll(one, LANES - shift, 1), two)
        for t in range(PLANES):
            sums[step, t] = held[t]
            rounded[step, t] = held[t].astype(jnp.bfloat16)
        for copy in onto(step):
            copy.start()

    half_rows = QUAD_ROWS // 2
    low_rows, high_rows = slice(0, half_rows), slice(half_rows, QUAD_ROWS)
    all_rows = slice(0, QUAD_ROWS)

    def reaches(chunk):
        one = high_rows if chunk < 2 else all_rows if chunk < 6 else low_rows
        two = None if chunk < 4 else high_rows if chunk < 6 else all_rows
        return one, two

    def finish(step):
        chunk = STEPS - 1 - step
        value = sums[step, plane]
        for n, copy in enumerate(onto(step)):
            copy.wait_recv()
            value = value + rounded_in[n, step].astype(jnp.float32)
        first = 16 * DISTANCES + chunk * CHUNK
        for k in range(CHUNK):
            extended[pl.ds(first + k, 8, stride=DISTANCES), :] = value[8 * k : 8 * k + 8]
        for k in range(0, 8, 2):
            both = [
                extended[pl.ds(pl.multiple_of(first + n * DISTANCES, CHUNK), CHUNK), :]
                for n in (k, k + 1)
            ]
            swap_out[chunk, 8 * k : 8 * k + 16] = jnp.concatenate(both, axis=0).astype(jnp.bfloat16)

        for low, high in ((0, 2), (2, 4), (4, 6), (6, 8)):

            @pl.when(jnp.logical_and(chunk >= low, chunk < high))
            def _():
                one, two = reaches(low)
                swap_copy(chunk, one, 1).start()
                if two is not None:
                    swap_copy(chunk, two, 2).start()

    def body(step, carry):
        def one(n, inner):
            fill(STEPS - 1 - step, 1 + n, CHUNK, weighted.at[n])
            return inner

        lax.fori_loop(0, TILES - 1, one, 0)
        value = times(weighted[0], 1)
        for n in range(1, TILES - 1):
            value = value + times(weighted[n], 1 + n)
        for h in range(2):
            part[step, h] += value[:, h * LANES : (h + 1) * LANES]
        pair_out[step] = part[step, 1 - core].astype(jnp.bfloat16)
        pair_copy(step).start()

        @pl.when(step >= 1)
        def _():
            forward(step - 1)

        @pl.when(step >= LAG)
        def _():
            finish(step - LAG)

        return carry

    lax.fori_loop(0, STEPS, body, 0)
    forward(STEPS - 1)

    columns = lax.broadcasted_iota(jnp.int32, (TOTAL, TOTAL), 1)
    for row in range(8):
        spot = jnp.where(placed[QUADS * row : QUADS * row + TOTAL, :] == columns, 1.0, 0.0)
        spots[row, :TOTAL] = spot.astype(jnp.bfloat16)
        spots[row, TOTAL:] = spot.astype(jnp.bfloat16)

    def last(step, carry):
        finish(step)
        return carry

    lax.fori_loop(STEPS - LAG, STEPS, last, 0)
    for step in range(STEPS):
        for copy in onto(step):
            copy.wait_send()

    quad = quad_of((8, LANES))

    def at_distance(d):
        if d > 0:
            return extended[pl.ds(16 * DISTANCES + d - 1, 8, stride=DISTANCES), :]
        if d == 0:
            return jnp.zeros((8, LANES), jnp.float32)
        row, rest = divmod(TOTAL // 2 + d, QUADS)
        value = extended[pl.ds(row * DISTANCES - d - 1, 8, stride=DISTANCES), :]
        if rest:
            later = extended[pl.ds((row + 1) * DISTANCES - d - 1, 8, stride=DISTANCES), :]
            value = pltpu.roll(jnp.where(quad >= rest, value, later), LANES - 32 * rest, 1)
        return -value

    def wrapped(d):
        return d - TOTAL if d > TOTAL // 2 else d

    def land(chunk):
        for reach, rows in enumerate(reaches(chunk), 1):
            if rows is None:
                continue
            swap_copy(chunk, rows, reach).wait()
            came = (swap_one if reach == 1 else swap_two)[chunk, rows].astype(jnp.float32)
            for n in range((rows.stop - rows.start) // 8):
                row = (2 - reach) * 8 + rows.start // 8 + n
                first = row * DISTANCES + chunk * CHUNK
                extended[first : first + CHUNK, :] = came[8 * n : 8 * n + 8]

    def place(first, stop):
        recent = [at_distance(wrapped(d)) for d in range(first - QUADS + 1, first)]
        for e in range(first, stop):
            recent.append(at_distance(wrapped(e)))
            value = recent[-1]
            for q in range(1, QUADS):
                value = jnp.where(quad == q, recent[-1 - q], value)
            row = e % TOTAL
            assembled[row * 8 : row * 8 + 8, :] = value

    for chunk in reversed(range(1, STEPS)):
        land(chunk)
    place(QUADS - TOTAL // 2, -CHUNK)
    place(QUADS, TOTAL // 2 + QUADS)
    land(0)
    place(-CHUNK, QUADS)

    for row in range(8):
        piece = assembled[pl.ds(row, TOTAL, stride=8), :].T
        high = piece.astype(jnp.bfloat16)
        low = (piece - high.astype(jnp.float32)).astype(jnp.bfloat16)
        moved = jnp.dot(
            jnp.concatenate([high, low], axis=1),
            spots[row],
            preferred_element_type=jnp.float32,
        )
        moved = moved * scale
        for q in range(QUADS):
            out_ref[pl.ds(QUADS * row + q, 32, stride=BLOCK), :] = moved[32 * q : 32 * q + 32]


def fast(vectors, momentum, assignment):
    mine = jnp.transpose(vectors, (0, 2, 1, 3))
    dma = pltpu.SemaphoreType.DMA
    f32, b16 = jnp.float32, jnp.bfloat16
    out = pl.pallas_call(
        fast_kernel,
        out_shape=jax.ShapeDtypeStruct((32 * BLOCK, TOTAL), f32),
        in_specs=[
            pl.BlockSpec(memory_space=pl.ANY),
            pl.BlockSpec(memory_space=pl.ANY),
            pl.BlockSpec(memory_space=pl.ANY),
        ],
        out_specs=pl.BlockSpec(memory_space=pltpu.VMEM),
        scratch_shapes=[
            pltpu.VMEM((1, TOTAL), jnp.int32),
            pltpu.SMEM((3,), jnp.int32),
            pltpu.VMEM((BLOCK, 3, 2, SITES), b16),
            pltpu.VMEM((TILES, 2, BLOCK, SLICE), b16),
            pltpu.VMEM((TILES, 2, GROUPS, BLOCK, 2 * SLICE), b16),
            pltpu.VMEM((9, TILES, QUADS, PART, LANES), f32),
            pltpu.VMEM((9, TILES, QUADS, 8, LANES), f32),
            pltpu.VMEM((2, TILES, 8, LANES), f32),
            pltpu.VMEM((2 * QUADS * PART + 2 * TOTAL, 2 * TOTAL), b16),
            pltpu.VMEM((TOTAL, LANES), jnp.int32),
            pltpu.VMEM((2 * TOTAL, LANES), jnp.int32),
            pltpu.VMEM((TILES - 1, CHUNK_ROWS, 2 * SLICE), b16),
            pltpu.VMEM((STEPS, 2, CHUNK_ROWS, LANES), f32),
            pltpu.VMEM((STEPS, CHUNK_ROWS, LANES), b16),
            pltpu.VMEM((STEPS, CHUNK_ROWS, LANES), b16),
            pltpu.VMEM((STEPS, PLANES, QUAD_ROWS, LANES), f32),
            pltpu.VMEM((STEPS, PLANES, QUAD_ROWS, LANES), b16),
            pltpu.VMEM((PLANES - 1, STEPS, QUAD_ROWS, LANES), b16),
            pltpu.VMEM((STEPS, QUAD_ROWS, LANES), b16),
            pltpu.VMEM((STEPS, QUAD_ROWS, LANES), b16),
            pltpu.VMEM((STEPS, QUAD_ROWS, LANES), b16),
            pltpu.VMEM((24 * DISTANCES, LANES), f32),
            pltpu.VMEM((8 * TOTAL, LANES), f32),
            pltpu.VMEM((8, 2 * TOTAL, TOTAL), b16),
            dma((3,)),
            dma,
            pltpu.SemaphoreType.REGULAR,
            dma((TILES, 6)),
            dma((TILES, 6)),
            dma((STEPS,)),
            dma((STEPS,)),
            dma((PLANES - 1, STEPS)),
            dma((PLANES - 1, STEPS)),
            dma((2, STEPS)),
            dma((2, STEPS)),
        ],
        compiler_params=pltpu.CompilerParams(
            collective_id=0, has_side_effects=True, vmem_limit_bytes=48 * 1024 * 1024
        ),
    )(assignment.reshape(1, TOTAL), momentum, mine)
    return out.reshape(16, 2, BLOCK, TOTAL)


def local(groups, spaces, vectors, momentum, assignment):
    if (groups, spaces) == (GROUPS, SPACES) and vectors.shape == (BLOCK, 2, 3, SITES):
        return fast(vectors, momentum, assignment)
    return general(groups, spaces, vectors, momentum, assignment)


def solution(mesh):
    return jax.shard_map(
        functools.partial(local, mesh.shape["group"], mesh.shape["space"]),
        mesh=mesh,
        in_specs=(P("group", None, None, "space"), P(), P()),
        out_specs=P("space", None, "group", None),
        check_vma=False,
    )
```
